32 devices in a mesh: px: 16 (over z, y, x), py: 2 (over core).
Axes of the slice: x: 2, y: 2, z: 4, core: 2. Of those that a mesh axis runs over, the one named last changes fastest.
Arguments:
- start_value: float32 [128, 256, 256], P(None, 'px', 'py'), may hold values from -6 to 6
- prior: float32 [128, 256, 256], P('px', None, 'py'), may hold values from -6 to 6
- reach: float32 [256, 256], P('px', 'py'), may hold values from -6 to 6
- avoid: float32 [256, 256], P('px', 'py'), may hold values from -3 to 0.5
Outputs:
- final_value: float32 [128, 256, 256], P(None, 'px', 'py')
The draws below stay inside these ranges and needn't reach their ends.
All inputs are finite; a program needn't handle non-finite values.
Results may differ from the reference program's by a relative error of at most 0.00002.
Values sent between devices are 32-bit elements; how exact they have to be, the bound alone decides.
No kernel may reach another device: no remote copies, remote signals or barrier semaphores. Data moves between devices by JAX's collectives and lax.ppermute only.
A program may use at most 64 MiB of HBM per device.

```python
import math
import jax
import jax.numpy as jnp
from jax import lax

NTH = 128
STEPS = 1
NX = 256
NY = 256


def level_of(key, dims, shards, least, top_value):
    factor_of = 1.0
    for position, parts in shards:
        steps = jax.random.uniform(jax.random.fold_in(jax.random.fold_in(key, 6), position), (parts,), jnp.float32, least / len(shards), top_value / len(shards))
        factor_of = factor_of * jnp.repeat(jnp.exp(steps), dims[position] // parts).reshape((-1,) + (1,) * (len(dims) - 1 - position))
    return factor_of


def normal_values(rng, dims, scale, most, cuts=(), kind=jnp.bfloat16):
    gain = level_of(rng, dims, cuts, -0.22, 0.18) if cuts else 1.0
    values = jax.random.normal(rng, dims, jnp.float32) * scale * gain
    return jnp.minimum(jnp.maximum(values, -most), most).astype(kind)


def setup_inputs(seed: int = 0) -> dict:
    streams_of = jax.random.split(jax.random.key(seed), 5)
    start_value = normal_values(streams_of[0], (NTH, NX, NY), 1.0, 6.0, ((1, 16), (2, 2)), jnp.float32)
    prior = normal_values(streams_of[1], (NTH, NX, NY), 1.0, 6.0, ((0, 16), (2, 2)), jnp.float32)
    reach = normal_values(streams_of[2], (NX, NY), 1.0, 6.0, ((0, 16), (1, 2)), jnp.float32)
    avoid = jnp.clip(-3.0 + 3.5 * jax.random.uniform(streams_of[3], (NX, NY), jnp.float32) ** level_of(streams_of[3], (NX, NY), ((0, 16), (1, 2)), -0.2, 0.2), -3.0, 0.5)
    return {"start_value": start_value, "prior": prior, "reach": reach, "avoid": avoid}


epsilon = 1e-6
spacing = 1.0 / 64.0
speed = 1.0
turn_rate = 2.0
courant = 0.5


def upwind_blend(first, second, third, fourth, fifth):
    stencil_one = first / 3.0 - 7.0 * second / 6.0 + 11.0 * third / 6.0
    stencil_two = -second / 6.0 + 5.0 * third / 6.0 + fourth / 3.0
    stencil_three = third / 3.0 + 5.0 * fourth / 6.0 - fifth / 6.0
    smooth_one = 13.0 / 12.0 * jnp.square(first - 2.0 * second + third) + 0.25 * jnp.square(first - 4.0 * second + 3.0 * third)
    smooth_two = 13.0 / 12.0 * jnp.square(second - 2.0 * third + fourth) + 0.25 * jnp.square(second - fourth)
    smooth_three = 13.0 / 12.0 * jnp.square(third - 2.0 * fourth + fifth) + 0.25 * jnp.square(3.0 * third - 4.0 * fourth + fifth)
    weight_one = 0.1 / jnp.square(epsilon + smooth_one)
    weight_two = 0.6 / jnp.square(epsilon + smooth_two)
    weight_three = 0.3 / jnp.square(epsilon + smooth_three)
    total = weight_one * stencil_one + weight_two * stencil_two + weight_three * stencil_three
    return total / (weight_one + weight_two + weight_three)


def one_sided(padded, along, length, width):
    slopes = (lax.slice_in_dim(padded, 1, length + 6, axis=along) - lax.slice_in_dim(padded, 0, length + 5, axis=along)) / width
    pieces = [lax.slice_in_dim(slopes, offset, offset + length, axis=along) for offset in range(6)]
    backward = upwind_blend(pieces[0], pieces[1], pieces[2], pieces[3], pieces[4])
    forward = upwind_blend(pieces[5], pieces[4], pieces[3], pieces[2], pieces[1])
    return backward, forward


def change_rate(extended):
    headings = extended.shape[0]
    row_count = extended.shape[1] - 6
    col_count = extended.shape[2] - 6
    heading_gap = 2.0 * math.pi / headings
    center = extended[:, 3:3 + row_count, 3:3 + col_count]
    west_slope, east_slope = one_sided(extended[:, :, 3:3 + col_count], 1, row_count, spacing)
    south_slope, north_slope = one_sided(extended[:, 3:3 + row_count, :], 2, col_count, spacing)
    wrapped = jnp.concatenate([center[headings - 3:], center, center[:3]], axis=0)
    right_slope, left_slope = one_sided(wrapped, 0, headings, heading_gap)
    angles = heading_gap * jnp.arange(headings, dtype=jnp.float32)
    cosine = jnp.cos(angles)[:, None, None]
    sine_value = jnp.sin(angles)[:, None, None]
    result = cosine * speed * 0.5 * (west_slope + east_slope) + sine_value * speed * 0.5 * (south_slope + north_slope)
    result = result - turn_rate * jnp.abs(0.5 * (right_slope + left_slope))
    result = result + speed * jnp.abs(cosine) * 0.5 * (east_slope - west_slope)
    result = result + speed * jnp.abs(sine_value) * 0.5 * (north_slope - south_slope)
    return result + turn_rate * 0.5 * (left_slope - right_slope)


def section_update(extended):
    headings = extended.shape[0]
    heading_gap = 2.0 * math.pi / headings
    time_step = courant / (2.0 * speed / spacing + turn_rate / heading_gap)
    center = extended[:, 3:extended.shape[1] - 3, 3:extended.shape[2] - 3]
    return center + time_step * change_rate(extended)


def advance(field):
    return section_update(jnp.pad(field, ((0, 0), (3, 3), (3, 3))))


def reference(start_value, prior, reach, avoid):
    values = start_value
    for step_index in range(STEPS):
        first = advance(values)
        second = 0.75 * values + 0.25 * advance(first)
        third = values / 3.0 + 2.0 / 3.0 * advance(second)
        values = jnp.minimum(prior, jnp.maximum(avoid[None], jnp.minimum(reach[None], third)))
    return values
```

```python
import functools
import math

import jax
import jax.numpy as jnp
import numpy as np
from jax import lax
from jax.experimental import pallas as pl
from jax.experimental.pallas import tpu as pltpu
from jax.sharding import PartitionSpec as P

EPS = 1e-06
SPACING = 1.0 / 64.0
SPEED = 1.0
TURN = 2.0
COURANT = 0.5
SCALE = 16.0
LANES = 128
SUB = 8
DEPTH = 9
OFF = 16


def ceil_div(a, b):
    return -(-a // b)


def stage_constants(headings, share):
    gap = 2.0 * math.pi / headings
    dt = COURANT / (2.0 * SPEED / SPACING + TURN / gap)
    angles = (np.float32(gap) * np.arange(headings, dtype=np.float32)).astype(np.float64)
    rows = []
    for wave in (np.cos(angles), np.sin(angles)):
        g = share * dt * SPEED * wave / SPACING
        ahead = wave >= 0
        rows += [
            g,
            np.where(ahead, -g / 3, g / 6),
            np.where(ahead, -g / 6, g / 3),
            np.where(ahead, 0.5, 1.0 / 6.0),
            np.where(ahead, 1.0 / 6.0, 0.5),
            np.where(ahead, g / 6, -g / 3),
            np.where(ahead, g / 3, -g / 6),
            np.where(ahead, 1.0, 0.0),
        ]
    turn = share * dt * TURN / (6.0 * gap)
    return np.stack(rows).astype(np.float32), float(turn)


def indicators(a, b, d, eps):
    bd = b * d
    ad = a * d
    ab = a * b
    mid = (bd - ad) * (2.0 / 3.0) + (ab * 0.5 + eps)
    return mid + bd, mid, mid - ad


def inverse(x):
    r = pl.reciprocal(x, approx=True)
    return r * (2.0 - x * r)


def sided(vals, coef, eps):
    n = len(vals)
    g, r2, r3, n1c, n3c, k1, k3 = coef
    u = [vals[i + 1] - vals[i] for i in range(n - 1)]
    w = [None] + [u[i] - u[i - 1] for i in range(1, n - 1)]
    d = [None] + [w[i + 1] - w[i] for i in range(1, n - 2)]
    tri = [None] + [indicators(w[i], w[i + 1], d[i], eps) for i in range(1, n - 2)]
    third = [None, None] + [d[i] - d[i - 1] for i in range(2, n - 2)]
    faces = {}
    for k in range(2, n - 3):
        low = tri[k - 1][0]
        mid = tri[k][1]
        high = tri[k + 1][2]
        mh = mid * high
        lh = low * high
        lm = low * mid
        m1 = (mh * mh) * n1c
        m2 = lh * lh
        m3 = (lm * lm) * n3c
        den = (m1 + m3) + m2
        num = m1 * (k1 * third[k]) + m3 * (k3 * third[k + 1])
        smooth = g * u[k] + r2 * w[k] + r3 * w[k + 1]
        faces[k] = smooth + num * inverse(den)
    return faces


def turning(v, eps):
    ahead = lambda x: pltpu.roll(x, LANES - 1, x.ndim - 1)
    behind = lambda x: pltpu.roll(x, 1, x.ndim - 1)
    u = ahead(v) - v
    w = u - behind(u)
    wn = ahead(w)
    d = wn - w
    low, mid, high = indicators(w, wn, d, eps)
    low = behind(low)
    high = ahead(high)
    g1 = d - behind(d)
    g2 = ahead(g1)
    mh = mid * high
    lh = low * high
    lm = low * mid
    m1 = mh * mh
    m2 = lh * lh
    m3 = lm * lm
    v0 = (m1 + m3) * 0.5 + m2 * 3.0
    a1 = m1 * g1
    a3 = m3 * g2
    s = w + wn
    top = u * 6.0 + wn + s
    back = (a1 + 1.5 * a3) * inverse(v0 + m3) - top
    fore = (top - 3.0 * s) + (a3 + 1.5 * a1) * inverse(v0 + m1)
    return jnp.minimum(behind(back), fore)


def prep_kernel(x_ref, o_ref):
    rows = o_ref.shape[0]
    for r in range(rows):
        o_ref[r] = x_ref[pl.ds(r, LANES, stride=rows), :].T * SCALE


def stage(src, dst, part, base, const_ref, lo, hi, seg, start, turn, eps_xy, eps_t, weights, row_of, rows_dst):
    def column(ref, row, j):
        return ref[row, pl.ds(OFF + start + j, SUB, stride=seg), :]

    def const(i):
        return const_ref[pl.ds(i, SUB, stride=0), :]

    xcoef = [const(i) for i in range(7)]
    ycoef = [const(i) for i in range(8, 15)]
    xmask = const(7) > 0.5
    ymask = const(15) > 0.5

    @pl.loop(0, seg)
    def _(j):
        vals = [column(src, row_of(r), j) for r in range(lo - 3, hi + 3)]
        faces = sided(vals, xcoef, eps_xy)
        for r in range(lo, hi):
            i = r - lo + 3
            move = jnp.where(xmask, faces[i], faces[i - 1])
            here = vals[i]
            if weights is not None:
                here = here * weights[0] + column(base, r + DEPTH, j) * weights[1]
            part[r - lo, j] = here + move

    @pl.loop(0, hi - lo)
    def _(r):
        vals = [column(src, row_of(lo) + r, j) for j in range(-3, seg + 3)]
        faces = sided(vals, ycoef, eps_xy)
        for j in range(seg):
            i = j + 3
            move = jnp.where(ymask, faces[i], faces[i - 1])
            out = part[r, j] + move + turn * turning(vals[i], eps_t)
            dst[r, pl.ds(OFF + start + j, SUB, stride=seg), :] = out


def main_kernel(edge_ref, const_ref, mid_ref, low_ref, high_ref, ylow_ref, yhigh_ref, o_ref, field, one, two, part, *, consts, sizes):
    rows, cols, headings = sizes
    gap = 2.0 * math.pi / headings
    eps_xy = 0.5 * EPS * (SCALE * SPACING) ** 2
    eps_t = 0.5 * EPS * (SCALE * gap) ** 2
    first_row = edge_ref[0] == 1
    last_row = edge_ref[1] == 1
    first_col = edge_ref[2] == 1
    last_col = edge_ref[3] == 1

    body = pl.ds(OFF, cols)
    field[pl.ds(0, DEPTH), body, :] = low_ref[...]
    field[pl.ds(DEPTH, rows), body, :] = mid_ref[...]
    field[pl.ds(DEPTH + rows, DEPTH), body, :] = high_ref[...]
    field[:, pl.ds(0, OFF), :] = ylow_ref[...]
    field[:, pl.ds(OFF + cols, OFF), :] = yhigh_ref[...]

    @pl.when(first_col)
    def _():
        field[:, pl.ds(0, OFF), :] = jnp.zeros((rows + 2 * DEPTH, OFF, LANES), jnp.float32)

    @pl.when(last_col)
    def _():
        field[:, pl.ds(OFF + cols, OFF), :] = jnp.zeros((rows + 2 * DEPTH, OFF, LANES), jnp.float32)

    def clear(ref, margin):
        count = rows + 2 * margin

        @pl.when(first_row)
        def _():
            ref[pl.ds(0, margin)] = jnp.zeros((margin,) + ref.shape[1:], jnp.float32)

        @pl.when(last_row)
        def _():
            ref[pl.ds(margin + rows, margin)] = jnp.zeros((margin,) + ref.shape[1:], jnp.float32)

        @pl.when(first_col)
        def _():
            ref[pl.ds(0, count), pl.ds(0, OFF), :] = jnp.zeros((count, OFF, LANES), jnp.float32)

        @pl.when(last_col)
        def _():
            ref[pl.ds(0, count), pl.ds(OFF + cols, OFF), :] = jnp.zeros((count, OFF, LANES), jnp.float32)

    def run(index, src, src_depth, dst, margin):
        seg = ceil_div(cols + 2 * margin, SUB)
        start = -((seg * SUB - cols) // 2)
        weights = (None, (0.25, 0.75), (2.0 / 3.0, 1.0 / 3.0))[index]
        stage(src, dst, part, field, const_ref.at[index], -margin, rows + margin, seg, start, consts[index],
              eps_xy, eps_t, weights, lambda r: r + src_depth, None)

    run(0, field, DEPTH, one, 6)
    clear(one, 6)
    run(1, one, 6, two, 3)
    clear(two, 3)
    run(2, two, 3, one, 0)
    for r in range(rows):
        o_ref[pl.ds(r, LANES, stride=rows), :] = one[r, pl.ds(OFF, cols), :].T * (1.0 / SCALE)


def on_device(start_value, prior, reach, avoid):
    headings, rows, cols = start_value.shape
    assert headings == LANES and cols == LANES
    regrouped = lax.all_to_all(prior, "px", split_axis=1, concat_axis=0, tiled=True)
    nx, ny = lax.axis_size("px"), lax.axis_size("py")
    px, py = lax.axis_index("px"), lax.axis_index("py")
    vmem = pl.BlockSpec(memory_space=pltpu.VMEM)
    f32 = jnp.float32
    mid = pl.pallas_call(
        prep_kernel,
        out_shape=jax.ShapeDtypeStruct((rows, cols, headings), f32),
        in_specs=[vmem],
        out_specs=vmem,
    )(start_value.reshape(headings * rows, cols))
    up = [(i, i + 1) for i in range(nx - 1)]
    down = [(b, a) for a, b in up]
    low = lax.ppermute(mid[rows - DEPTH :], "px", up)
    high = lax.ppermute(mid[:DEPTH], "px", down)
    if ny == 2:
        swap = [(0, 1), (1, 0)]
        first = py == 0
        column = lambda x: jnp.where(first, x[:, cols - OFF :], x[:, :OFF])
        slab = jnp.concatenate([column(low), column(mid), column(high)], axis=0)
        ylow = yhigh = lax.ppermute(slab, "py", swap)
    else:
        yup = [(i, i + 1) for i in range(ny - 1)]
        ydown = [(b, a) for a, b in yup]
        full = jnp.concatenate([low, mid, high], axis=0)
        ylow = lax.ppermute(full[:, cols - OFF :], "py", yup)
        yhigh = lax.ppermute(full[:, :OFF], "py", ydown)
    edges = jnp.stack([px == 0, px == nx - 1, py == 0, py == ny - 1]).astype(jnp.int32)
    tables = [stage_constants(headings, share) for share in (1.0, 0.25, 2.0 / 3.0)]
    table = jnp.asarray(np.stack([t[0] for t in tables]))
    seg = ceil_div(cols + 12, SUB)
    tall = rows + 2 * DEPTH
    wide = cols + 2 * OFF
    third = pl.pallas_call(
        functools.partial(main_kernel, consts=[t[1] for t in tables], sizes=(rows, cols, headings)),
        out_shape=jax.ShapeDtypeStruct((headings * rows, cols), f32),
        in_specs=[pl.BlockSpec(memory_space=pltpu.SMEM)] + [vmem] * 6,
        out_specs=vmem,
        scratch_shapes=[
            pltpu.VMEM((tall, wide, LANES), f32),
            pltpu.VMEM((rows + 12, wide, LANES), f32),
            pltpu.VMEM((rows + 6, wide, LANES), f32),
            pltpu.VMEM((rows + 12, seg, SUB, LANES), f32),
        ],
        compiler_params=pltpu.CompilerParams(vmem_limit_bytes=40 * 2**20),
    )(edges, table, mid, low, high, ylow, yhigh).reshape(headings, rows, cols)
    return jnp.minimum(regrouped, jnp.maximum(avoid[None], jnp.minimum(reach[None], third)))


def solution(mesh):
    return jax.shard_map(
        on_device,
        mesh=mesh,
        in_specs=(P(None, "px", "py"), P("px", None, "py"), P("px", "py"), P("px", "py")),
        out_specs=P(None, "px", "py"),
        check_vma=False,
    )
```

```python
import functools
import math

import jax
import jax.numpy as jnp
import numpy as np
from jax import lax
from jax.experimental import pallas as pl
from jax.experimental.pallas import tpu as pltpu
from jax.sharding import PartitionSpec as P

EPS = 1e-06
SPACING = 1.0 / 64.0
SPEED = 1.0
TURN = 2.0
COURANT = 0.5
LANES = 128
SUB = 8
DEPTH = 9
OFF = 16


def ceil_div(a, b):
    return -(-a // b)


def stage_constants(headings, share):
    gap = 2.0 * math.pi / headings
    dt = COURANT / (2.0 * SPEED / SPACING + TURN / gap)
    angles = (np.float32(gap) * np.arange(headings, dtype=np.float32)).astype(np.float64)
    rows = []
    for wave in (np.cos(angles), np.sin(angles)):
        g = share * dt * SPEED * wave / SPACING
        ahead = wave >= 0
        rows += [
            g,
            np.where(ahead, -g / 3, g / 6),
            np.where(ahead, -g / 6, g / 3),
            np.where(ahead, 0.5, 1.0 / 6.0),
            np.where(ahead, 1.0 / 6.0, 0.5),
            np.where(ahead, g / 6, -g / 3),
            np.where(ahead, g / 3, -g / 6),
            np.where(ahead, 1.0, 0.0),
        ]
    turn = share * dt * TURN / (6.0 * gap)
    return np.stack(rows).astype(np.float32), float(turn)


def weights_of(a, b, d, eps, want):
    bd = b * d
    ad = a * d
    ab = a * b
    mid = (bd - ad) * (2.0 / 3.0) + (ab * 0.5 + eps)
    out = []
    for name in want:
        x = {"L": mid + bd if "L" in want else None, "C": mid, "R": mid - ad if "R" in want else None}[name]
        r = inverse(x)
        out.append(r * r)
    return out


def inverse(x):
    return 1.0 / x


def sided(vals, coef, eps):
    n = len(vals)
    g, r2, r3, n1c, n3c, k1, k3 = coef
    u = [vals[i + 1] - vals[i] for i in range(n - 1)]
    w = [None] + [u[i] - u[i - 1] for i in range(1, n - 1)]
    d = [None] + [w[i + 1] - w[i] for i in range(1, n - 2)]
    tri = [None] + [weights_of(w[i], w[i + 1], d[i], eps, "LCR") for i in range(1, n - 2)]
    third = [None, None] + [d[i] - d[i - 1] for i in range(2, n - 2)]
    faces = {}
    for k in range(2, n - 3):
        m1 = tri[k - 1][0] * n1c
        m2 = tri[k][1]
        m3 = tri[k + 1][2] * n3c
        den = (m1 + m3) + m2
        num = m1 * (k1 * third[k]) + m3 * (k3 * third[k + 1])
        smooth = g * u[k] + r2 * w[k] + r3 * w[k + 1]
        faces[k] = smooth + num * inverse(den)
    return faces


def turning(v, eps):
    ahead = lambda x: pltpu.roll(x, LANES - 1, x.ndim - 1)
    behind = lambda x: pltpu.roll(x, 1, x.ndim - 1)
    u = ahead(v) - v
    w = u - behind(u)
    wn = ahead(w)
    d = wn - w
    low, mid, high = weights_of(w, wn, d, eps, "LCR")
    m1 = behind(low)
    m3 = ahead(high)
    g1 = d - behind(d)
    g2 = ahead(g1)
    v0 = (m1 + m3) * 0.5 + mid * 3.0
    a1 = m1 * g1
    a3 = m3 * g2
    s = w + wn
    top = u * 6.0 + wn + s
    back = (a1 + 1.5 * a3) * inverse(v0 + m3) - top
    fore = (top - 3.0 * s) + (a3 + 1.5 * a1) * inverse(v0 + m1)
    return jnp.minimum(behind(back), fore)


def lanes_of(shape):
    return lax.broadcasted_iota(jnp.int32, shape, len(shape) - 1)


def fold(rows, shift):
    half = rows.shape[0] // 2
    low = pltpu.roll(rows[:half], (-shift) % LANES, 1)
    high = pltpu.roll(rows[half:], shift % LANES, 1)
    return jnp.where(lanes_of(low.shape) < LANES // 2, low, high)


def unfold(packed, shift):
    return pltpu.roll(packed, shift % LANES, 1), pltpu.roll(packed, (-shift) % LANES, 1)


QUARTER = LANES // 4
FULL = 6


def prep_kernel(x_ref, mid_ref, one_ref, two_ref):
    rows, cols = mid_ref.shape[:2]
    half = cols // 2
    for r in range(rows):
        mid_ref[r] = x_ref[pl.ds(r, LANES, stride=rows), :].T

    def upper(ref):
        for i in range(FULL):
            ref[pl.ds(i * cols, cols), :] = mid_ref[rows - FULL + i]
        for i in range(3):
            ref[pl.ds(FULL * cols + i * half, half), :] = fold(mid_ref[rows - FULL - 3 + i], QUARTER)

    def lower(ref):
        for i in range(FULL):
            ref[pl.ds(i * cols, cols), :] = mid_ref[i]
        for i in range(3):
            ref[pl.ds(FULL * cols + i * half, half), :] = fold(mid_ref[FULL + i], -QUARTER)

    even = lax.rem(lax.axis_index("px"), 2) == 0

    @pl.when(even)
    def _():
        upper(one_ref)
        lower(two_ref)

    @pl.when(jnp.logical_not(even))
    def _():
        lower(one_ref)
        upper(two_ref)


def halo_parts(low, one_ref, two_ref, rows, cols, write):
    half = cols // 2

    def emit(ref):
        for i in range(FULL):
            write(3 + i if low else DEPTH + rows + i, 0, ref[pl.ds(i * cols, cols), :])
        for i in range(3):
            packed = ref[pl.ds(FULL * cols + i * half, half), :]
            row = i if low else DEPTH + rows + FULL + i
            a, b = unfold(packed, QUARTER if low else -QUARTER)
            write(row, 0, a)
            write(row, half, b)

    even = lax.rem(lax.axis_index("px"), 2) == 0
    first, second = (two_ref, one_ref) if low else (one_ref, two_ref)

    @pl.when(even)
    def _():
        emit(first)

    @pl.when(jnp.logical_not(even))
    def _():
        emit(second)


def edge_kernel(mid_ref, one_ref, two_ref, *slabs, sides):
    rows, cols = mid_ref.shape[:2]

    def fill(ref, right):
        begin = cols - OFF if right else 0
        ref[pl.ds(DEPTH, rows)] = mid_ref[:, pl.ds(begin, OFF), :]

        def write(row, col, values):
            count = values.shape[0]
            if col <= begin and begin + OFF <= col + count:
                ref[row] = values[begin - col : begin - col + OFF]

        halo_parts(True, one_ref, two_ref, rows, cols, write)
        halo_parts(False, one_ref, two_ref, rows, cols, write)

    if sides == 1:
        at_left = lax.axis_index("py") == 0

        @pl.when(at_left)
        def _():
            fill(slabs[0], True)

        @pl.when(jnp.logical_not(at_left))
        def _():
            fill(slabs[0], False)
    else:
        fill(slabs[0], True)
        fill(slabs[1], False)


def zpack_kernel(p_ref, *outs, inner):
    z = lax.axis_index("px") // inner
    rows = outs[0].shape[2]
    for k, out in enumerate(outs):
        for q in range(inner):
            start = ((z ^ k) * inner + q) * rows
            out[q] = p_ref[:, pl.ds(pl.multiple_of(start, rows), rows), :]


def qpack_kernel(*refs, inner, outer):
    ins, outs = refs[:outer], refs[outer:]
    q = lax.rem(lax.axis_index("px"), inner)
    for m, out in enumerate(outs):
        for k in range(outer):
            out[k] = ins[k][q ^ m]


def final_kernel(third_ref, reach_ref, avoid_ref, *refs, inner, outer):
    ins, o_ref = refs[:inner], refs[inner]
    px = lax.axis_index("px")
    z, q = px // inner, lax.rem(px, inner)
    count = ins[0].shape[1]
    reach, avoid = reach_ref[...], avoid_ref[...]
    for m in range(inner):
        for k in range(outer):
            block = pl.ds(((z ^ k) * inner + (q ^ m)) * count, count)
            kept = jnp.maximum(avoid[None], jnp.minimum(reach[None], third_ref[block]))
            o_ref[block] = jnp.minimum(ins[m][k], kept)


def stage(src, dst, part, base, const_ref, lo, hi, seg, start, turn, eps_xy, eps_t, weights, depth):
    def column(ref, row, j):
        return ref[row, pl.ds(OFF + start + j, SUB, stride=seg), :]

    def const(i):
        return const_ref[pl.ds(i, SUB, stride=0), :]

    xcoef = [const(i) for i in range(7)]
    ycoef = [const(i) for i in range(8, 15)]
    xmask = const(7) > 0.5
    ymask = const(15) > 0.5

    @pl.loop(0, seg)
    def _(j):
        vals = [column(src, r + depth, j) for r in range(lo - 3, hi + 3)]
        faces = sided(vals, xcoef, eps_xy)
        for r in range(lo, hi):
            i = r - lo + 3
            move = jnp.where(xmask, faces[i], faces[i - 1])
            here = vals[i]
            if weights is not None:
                here = here * weights[0] + column(base, r + DEPTH, j) * weights[1]
            part[r - lo, j] = here + move

    @pl.loop(0, hi - lo)
    def _(r):
        vals = [column(src, lo + depth + r, j) for j in range(-3, seg + 3)]
        faces = sided(vals, ycoef, eps_xy)
        for j in range(seg):
            i = j + 3
            move = jnp.where(ymask, faces[i], faces[i - 1])
            out = part[r, j] + move + turn * turning(vals[i], eps_t)
            dst[r, pl.ds(OFF + start + j, SUB, stride=seg), :] = out


def main_kernel(const_ref, mid_ref, recv1_ref, recv2_ref, ylow_ref, yhigh_ref, o_ref, field, one, two, part, *, consts, sizes):
    rows, cols, headings = sizes
    gap = 2.0 * math.pi / headings
    eps_xy = 0.5 * EPS * SPACING**2
    eps_t = 0.5 * EPS * gap**2
    px, py = lax.axis_index("px"), lax.axis_index("py")
    first_row = px == 0
    last_row = px == lax.axis_size("px") - 1
    first_col = py == 0
    last_col = py == lax.axis_size("py") - 1
    tall = rows + 2 * DEPTH

    def write(row, col, values):
        field[row, pl.ds(OFF + col, values.shape[0]), :] = values

    field[pl.ds(DEPTH, rows), pl.ds(OFF, cols), :] = mid_ref[...]
    halo_parts(True, recv1_ref, recv2_ref, rows, cols, write)
    halo_parts(False, recv1_ref, recv2_ref, rows, cols, write)
    for at_edge, begin, slab in ((first_col, 0, ylow_ref), (last_col, OFF + cols, yhigh_ref)):

        @pl.when(at_edge)
        def _():
            field[:, pl.ds(begin, OFF), :] = jnp.zeros((tall, OFF, LANES), jnp.float32)

        @pl.when(jnp.logical_not(at_edge))
        def _():
            field[:, pl.ds(begin, OFF), :] = slab[...]

    def clear(ref, margin):
        count = rows + 2 * margin

        @pl.when(first_row)
        def _():
            ref[pl.ds(0, margin)] = jnp.zeros((margin,) + ref.shape[1:], jnp.float32)

        @pl.when(last_row)
        def _():
            ref[pl.ds(margin + rows, margin)] = jnp.zeros((margin,) + ref.shape[1:], jnp.float32)

        @pl.when(first_col)
        def _():
            ref[pl.ds(0, count), pl.ds(0, OFF), :] = jnp.zeros((count, OFF, LANES), jnp.float32)

        @pl.when(last_col)
        def _():
            ref[pl.ds(0, count), pl.ds(OFF + cols, OFF), :] = jnp.zeros((count, OFF, LANES), jnp.float32)

    def run(index, src, src_depth, dst, margin):
        seg = ceil_div(cols + 2 * margin, SUB)
        start = -((seg * SUB - cols) // 2)
        weights = (None, (0.25, 0.75), (2.0 / 3.0, 1.0 / 3.0))[index]
        stage(src, dst, part, field, const_ref.at[index], -margin, rows + margin, seg, start, consts[index],
              eps_xy, eps_t, weights, src_depth)

    run(0, field, DEPTH, one, 6)
    clear(one, 6)
    run(1, one, 6, two, 3)
    clear(two, 3)
    run(2, two, 3, one, 0)
    for r in range(rows):
        o_ref[pl.ds(r, LANES, stride=rows), :] = one[r, pl.ds(OFF, cols), :].T


def on_device(start_value, prior, reach, avoid):
    headings, rows, cols = start_value.shape
    nx, ny = lax.axis_size("px"), lax.axis_size("py")
    inner = 4 if nx % 4 == 0 else 1
    outer = nx // inner
    assert headings == LANES and cols == LANES and rows >= DEPTH
    assert nx % 2 == 0 and outer & (outer - 1) == 0
    f32 = jnp.float32
    vmem = pl.BlockSpec(memory_space=pltpu.VMEM)

    def call(kernel, outs, *args, **kw):
        return pl.pallas_call(
            kernel,
            out_shape=[jax.ShapeDtypeStruct(o, f32) for o in outs],
            in_specs=[vmem] * len(args),
            out_specs=[vmem] * len(outs),
            **kw,
        )(*args)

    message = (FULL * cols + 3 * cols // 2, headings)
    mid, send1, send2 = call(
        prep_kernel, [(rows, cols, headings), message, message], start_value.reshape(headings * rows, cols)
    )
    pairs1 = [(i, i ^ 1) for i in range(nx)]
    pairs2 = [(i, j) for i in range(nx) for j in [((i + 1) ^ 1) - 1] if 0 <= j < nx]
    recv1 = lax.ppermute(send1, "px", pairs1)
    recv2 = lax.ppermute(send2, "px", pairs2)

    share = (inner, headings // nx, rows, cols)
    zsend = call(functools.partial(zpack_kernel, inner=inner), [share] * outer, prior)
    zrecv = [zsend[0]] + [
        lax.ppermute(zsend[k], "px", [(i, ((i // inner) ^ k) * inner + i % inner) for i in range(nx)])
        for k in range(1, outer)
    ]

    sides = 1 if ny == 2 else 2
    slabs = call(
        functools.partial(edge_kernel, sides=sides), [(rows + 2 * DEPTH, OFF, headings)] * sides, mid, recv1, recv2
    )
    if sides == 1:
        ylow = yhigh = lax.ppermute(slabs[0], "py", [(0, 1), (1, 0)])
    else:
        ylow = lax.ppermute(slabs[0], "py", [(i, i + 1) for i in range(ny - 1)])
        yhigh = lax.ppermute(slabs[1], "py", [(i + 1, i) for i in range(ny - 1)])

    share = (outer, headings // nx, rows, cols)
    qsend = call(functools.partial(qpack_kernel, inner=inner, outer=outer), [share] * inner, *zrecv)
    qrecv = [qsend[0]] + [
        lax.ppermute(qsend[m], "px", [(i, (i // inner) * inner + ((i % inner) ^ m)) for i in range(nx)])
        for m in range(1, inner)
    ]

    tables = [stage_constants(headings, part) for part in (1.0, 0.25, 2.0 / 3.0)]
    table = jnp.asarray(np.stack([t[0] for t in tables]))
    seg = ceil_div(cols + 12, SUB)
    wide = cols + 2 * OFF
    (third,) = call(
        functools.partial(main_kernel, consts=[t[1] for t in tables], sizes=(rows, cols, headings)),
        [(headings * rows, cols)],
        table, mid, recv1, recv2, ylow, yhigh,
        scratch_shapes=[
            pltpu.VMEM((rows + 2 * DEPTH, wide, LANES), f32),
            pltpu.VMEM((rows + 12, wide, LANES), f32),
            pltpu.VMEM((rows + 6, wide, LANES), f32),
            pltpu.VMEM((rows + 12, seg, SUB, LANES), f32),
        ],
        compiler_params=pltpu.CompilerParams(vmem_limit_bytes=40 * 2**20),
    )
    (out,) = call(
        functools.partial(final_kernel, inner=inner, outer=outer),
        [(headings, rows, cols)],
        third.reshape(headings, rows, cols), reach, avoid, *qrecv,
    )
    return out


def solution(mesh):
    return jax.shard_map(
        on_device,
        mesh=mesh,
        in_specs=(P(None, "px", "py"), P("px", None, "py"), P("px", "py"), P("px", "py")),
        out_specs=P(None, "px", "py"),
        check_vma=False,
    )
```

```python
import functools
import math

import jax
import jax.numpy as jnp
import numpy as np
from jax import lax
from jax.experimental import pallas as pl
from jax.experimental.pallas import tpu as pltpu
from jax.sharding import PartitionSpec as P

EPS = 1e-06
SPACING = 1.0 / 64.0
SPEED = 1.0
TURN = 2.0
COURANT = 0.5
LANES = 128
SUB = 8
DEPTH = 6
OFF = 16


LIMIT = 12


def ceil_div(a, b):
    return -(-a // b)


def stage_constants(headings, share):
    gap = 2.0 * math.pi / headings
    dt = COURANT / (2.0 * SPEED / SPACING + TURN / gap)
    angles = (np.float32(gap) * np.arange(headings, dtype=np.float32)).astype(np.float64)
    rows = []
    for wave in (np.cos(angles), np.sin(angles)):
        g = share * dt * SPEED * wave / SPACING
        ahead = wave >= 0
        rows += [
            g,
            np.where(ahead, -g / 3, g / 6),
            np.where(ahead, -g / 6, g / 3),
            np.where(ahead, 0.5, 1.0 / 6.0),
            np.where(ahead, 1.0 / 6.0, 0.5),
            np.where(ahead, g / 6, -g / 3),
            np.where(ahead, g / 3, -g / 6),
            np.where(ahead, 1.0, 0.0),
        ]
    turn = share * dt * TURN / (6.0 * gap)
    return np.stack(rows).astype(np.float32), float(turn)


def weights_of(a, b, d, eps, want):
    bd = b * d
    ad = a * d
    ab = a * b
    mid = (bd - ad) * (2.0 / 3.0) + (ab * 0.5 + eps)
    out = []
    for name in want:
        x = {"L": mid + bd if "L" in want else None, "C": mid, "R": mid - ad if "R" in want else None}[name]
        r = inverse(x)
        out.append(r * r)
    return out


def inverse(x):
    return 1.0 / x


def sided(vals, coef, eps):
    n = len(vals)
    g, r2, r3, n1c, n3c, k1, k3 = coef
    u = [vals[i + 1] - vals[i] for i in range(n - 1)]
    w = [None] + [u[i] - u[i - 1] for i in range(1, n - 1)]
    d = [None] + [w[i + 1] - w[i] for i in range(1, n - 2)]
    tri = [None] + [weights_of(w[i], w[i + 1], d[i], eps, "LCR") for i in range(1, n - 2)]
    third = [None, None] + [d[i] - d[i - 1] for i in range(2, n - 2)]
    faces = {}
    for k in range(2, n - 3):
        m1 = tri[k - 1][0] * n1c
        m2 = tri[k][1]
        m3 = tri[k + 1][2] * n3c
        den = (m1 + m3) + m2
        num = m1 * (k1 * third[k]) + m3 * (k3 * third[k + 1])
        smooth = g * u[k] + r2 * w[k] + r3 * w[k + 1]
        faces[k] = smooth + num * inverse(den)
    return faces


def turning(v, eps):
    ahead = lambda x: pltpu.roll(x, LANES - 1, x.ndim - 1)
    behind = lambda x: pltpu.roll(x, 1, x.ndim - 1)
    u = ahead(v) - v
    w = u - behind(u)
    wn = ahead(w)
    d = wn - w
    low, mid, high = weights_of(w, wn, d, eps, "LCR")
    m1 = behind(low)
    m3 = ahead(high)
    g1 = d - behind(d)
    g2 = ahead(g1)
    v0 = (m1 + m3) * 0.5 + mid * 3.0
    a1 = m1 * g1
    a3 = m3 * g2
    s = w + wn
    top = u * 6.0 + wn + s
    back = (a1 + 1.5 * a3) * inverse(v0 + m3) - top
    fore = (top - 3.0 * s) + (a3 + 1.5 * a1) * inverse(v0 + m1)
    return jnp.minimum(behind(back), fore)


def lanes_of(shape):
    return lax.broadcasted_iota(jnp.int32, shape, len(shape) - 1)


def fold(rows, shift):
    half = rows.shape[0] // 2
    low = pltpu.roll(rows[:half], (-shift) % LANES, 1)
    high = pltpu.roll(rows[half:], shift % LANES, 1)
    return jnp.where(lanes_of(low.shape) < LANES // 2, low, high)


def unfold(packed, shift):
    return pltpu.roll(packed, shift % LANES, 1), pltpu.roll(packed, (-shift) % LANES, 1)


QUARTER = LANES // 4
FULL1, HALF1 = 4, 2
FULL2, HALF2 = 2, 1


def even_tile():
    return lax.rem(lax.axis_index("px"), 2) == 0


def pack(ref, read, count, full, half):
    for i in range(full):
        ref[pl.ds(i * count, count), :] = read(i)[0]
    for i in range(half):
        values, shift = read(full + i)
        ref[pl.ds(full * count + i * (count // 2), count // 2), :] = fold(values, shift)


def pack_pair(one_ref, two_ref, row, rows, count, full, half):
    upper = lambda i: (row(rows - 1 - i), QUARTER)
    lower = lambda i: (row(i), -QUARTER)

    @pl.when(even_tile())
    def _():
        pack(one_ref, upper, count, full, half)
        pack(two_ref, lower, count, full, half)

    @pl.when(jnp.logical_not(even_tile()))
    def _():
        pack(one_ref, lower, count, full, half)
        pack(two_ref, upper, count, full, half)


def unpack_pair(one_ref, two_ref, write, rows, count, full, half):
    def unpack(ref, low):
        at = lambda i: -1 - i if low else rows + i
        for i in range(full):
            write(at(i), 0, ref[pl.ds(i * count, count), :])
        for i in range(half):
            packed = ref[pl.ds(full * count + i * (count // 2), count // 2), :]
            first, second = unfold(packed, QUARTER if low else -QUARTER)
            write(at(full + i), 0, first)
            write(at(full + i), count // 2, second)

    @pl.when(even_tile())
    def _():
        unpack(one_ref, False)
        unpack(two_ref, True)

    @pl.when(jnp.logical_not(even_tile()))
    def _():
        unpack(one_ref, True)
        unpack(two_ref, False)


def prep_kernel(x_ref, mid_ref, one_ref, two_ref, *slabs):
    rows, cols = mid_ref.shape[:2]
    for r in range(rows):
        mid_ref[r] = x_ref[pl.ds(r, LANES, stride=rows), :].T
    pack_pair(one_ref, two_ref, lambda r: mid_ref[r], rows, cols, FULL1, HALF1)
    right = lambda ref: ref.__setitem__(Ellipsis, mid_ref[:, pl.ds(cols - OFF, OFF), :])
    left = lambda ref: ref.__setitem__(Ellipsis, mid_ref[:, pl.ds(0, OFF), :])
    if len(slabs) == 1:
        pl.when(lax.axis_index("py") == 0)(lambda: right(slabs[0]))
        pl.when(lax.axis_index("py") != 0)(lambda: left(slabs[0]))
    else:
        right(slabs[0])
        left(slabs[1])


def spread_kernel(p_ref, o_ref):
    rows = o_ref.shape[2]
    for i in range(o_ref.shape[0]):
        o_ref[i] = p_ref[:, pl.ds(i * rows, rows), :]


def columns_of(cols, margin):
    seg = ceil_div(cols + 2 * margin, SUB)
    return seg, -((seg * SUB - cols) // 2)


def stage(index, src, dst, base, part, const_ref, parts, sizes, turn):
    cols, margin, gap = sizes
    seg, start = columns_of(cols, margin)
    eps_xy = 0.5 * EPS * SPACING**2
    eps_t = 0.5 * EPS * gap**2
    weights = (None, (0.25, 0.75), (2.0 / 3.0, 1.0 / 3.0))[index]

    def column(array, row, j):
        return array[0][row + array[1], pl.ds(OFF + start + j, SUB, stride=seg), :]

    def const(i):
        return const_ref[index, pl.ds(i, SUB, stride=0), :]

    xcoef = [const(i) for i in range(7)]
    ycoef = [const(i) for i in range(8, 15)]
    xmask = const(7) > 0.5
    ymask = const(15) > 0.5

    @pl.loop(0, seg)
    def _(j):
        at = 0
        for lo, hi in parts:
            vals = [column(src, r, j) for r in range(lo - 3, hi + 3)]
            faces = sided(vals, xcoef, eps_xy)
            for r in range(lo, hi):
                i = r - lo + 3
                move = jnp.where(xmask, faces[i], faces[i - 1])
                here = vals[i]
                if weights is not None:
                    here = here * weights[0] + column(base, r, j) * weights[1]
                part[at, j] = here + move
                at += 1

    counts = [hi - lo for lo, hi in parts]

    @pl.loop(0, sum(counts))
    def _(t):
        row = t + parts[0][0]
        if len(parts) == 2:
            row = jnp.where(t < counts[0], row, t - counts[0] + parts[1][0])
        vals = [column(src, row, j) for j in range(-3, seg + 3)]
        faces = sided(vals, ycoef, eps_xy)
        for j in range(seg):
            i = j + 3
            move = jnp.where(ymask, faces[i], faces[i - 1])
            out = part[t, j] + move + turn * turning(vals[i], eps_t)
            dst[0][row + dst[1], pl.ds(OFF + start + j, SUB, stride=seg), :] = out


def clear_columns(dst, parts, cols):
    py = lax.axis_index("py")
    for edge, begin in ((0, 0), (lax.axis_size("py") - 1, OFF + cols)):

        @pl.when(py == edge)
        def _():
            for lo, hi in parts:
                dst[0][pl.ds(lo + dst[1], hi - lo), pl.ds(begin, OFF), :] = jnp.zeros((hi - lo, OFF, LANES), jnp.float32)


def inner_kernel(const_ref, mid_ref, ylow_ref, yhigh_ref, field, one, part, *, turns, gap):
    rows, cols = mid_ref.shape[:2]
    own = pl.ds(DEPTH, rows)
    field[own, pl.ds(OFF, cols), :] = mid_ref[...]
    field[own, pl.ds(0, OFF), :] = ylow_ref[...]
    field[own, pl.ds(OFF + cols, OFF), :] = yhigh_ref[...]
    clear_columns((field, DEPTH), [(0, rows)], cols)
    parts = [(3, rows - 3)]
    stage(0, (field, DEPTH), (one, 3), None, part, const_ref, parts, (cols, 6, gap), turns[0])
    clear_columns((one, 3), parts, cols)


def outer_kernel(const_ref, recv1_ref, recv2_ref, side1_ref, side2_ref, field_in, one_in, field, one, two, send1, send2, part, *, turns, gap, rows, cols):
    del field_in, one_in

    def write(row, col, values):
        field[row + DEPTH, pl.ds(OFF + col, values.shape[0]), :] = values

    unpack_pair(recv1_ref, recv2_ref, write, rows, cols, FULL1, HALF1)
    low, high = pl.ds(0, DEPTH), pl.ds(DEPTH + rows, DEPTH)

    def sides(ref, where):
        field[where, pl.ds(0, OFF), :] = ref[0]
        field[where, pl.ds(OFF + cols, OFF), :] = ref[ref.shape[0] - 1]

    @pl.when(even_tile())
    def _():
        sides(side1_ref, high)
        sides(side2_ref, low)

    @pl.when(jnp.logical_not(even_tile()))
    def _():
        sides(side1_ref, low)
        sides(side2_ref, high)

    clear_columns((field, DEPTH), [(-DEPTH, 0), (rows, rows + DEPTH)], cols)
    parts = [(-3, 3), (rows - 3, rows + 3)]
    stage(0, (field, DEPTH), (one, 3), None, part, const_ref, parts, (cols, 6, gap), turns[0])
    clear_columns((one, 3), parts, cols)
    px = lax.axis_index("px")
    for edge, begin in ((0, 0), (lax.axis_size("px") - 1, 3 + rows)):

        @pl.when(px == edge)
        def _():
            one[pl.ds(begin, 3)] = jnp.zeros((3,) + one.shape[1:], jnp.float32)

    parts = [(0, 3), (rows - 3, rows)]
    stage(1, (one, 3), (two, 3), (field, DEPTH), part, const_ref, parts, (cols, 3, gap), turns[1])
    clear_columns((two, 3), parts, cols)
    seg, start = columns_of(cols, 3)
    count = seg * SUB
    pack_pair(send1, send2, lambda r: two[r + 3, pl.ds(OFF + start, count), :], rows, count, FULL2, HALF2)


def middle_kernel(const_ref, field, one, two_in, two, three, part, *, turns, gap, rows, cols):
    del two_in
    parts = [(3, rows - 3)]
    stage(1, (one, 3), (two, 3), (field, DEPTH), part, const_ref, parts, (cols, 3, gap), turns[1])
    clear_columns((two, 3), parts, cols)
    stage(2, (two, 3), (three, 0), (field, DEPTH), part, const_ref, parts, (cols, 0, gap), turns[2])


def last_kernel(const_ref, recv1_ref, recv2_ref, field, two_in, three_in, prior_ref, reach_ref, avoid_ref, o_ref, two, three, part, *, turns, gap, rows, cols):
    del two_in, three_in
    seg, start = columns_of(cols, 3)

    def write(row, col, values):
        two[row + 3, pl.ds(OFF + start + col, values.shape[0]), :] = values

    unpack_pair(recv1_ref, recv2_ref, write, rows, seg * SUB, FULL2, HALF2)
    parts = [(0, 3), (rows - 3, rows)]
    stage(2, (two, 3), (three, 0), (field, DEPTH), part, const_ref, parts, (cols, 0, gap), turns[2])
    for r in range(rows):
        lines = pl.ds(r, LANES, stride=rows)
        value = three[r, pl.ds(OFF, cols), :].T
        kept = jnp.maximum(avoid_ref[pl.ds(r, LANES, stride=0), :], jnp.minimum(reach_ref[pl.ds(r, LANES, stride=0), :], value))
        o_ref[lines, :] = jnp.minimum(prior_ref[lines, :], kept)


def on_device(start_value, prior, reach, avoid):
    headings, rows, cols = start_value.shape
    nx, ny = lax.axis_size("px"), lax.axis_size("py")
    assert headings == LANES and cols == LANES and rows >= 2 * DEPTH and nx % 2 == 0
    gap = 2.0 * math.pi / headings
    f32 = jnp.float32
    vmem = pl.BlockSpec(memory_space=pltpu.VMEM)

    def call(kernel, outs, *args, limit=LIMIT, aliases={}, scratch=(), **kw):
        return pl.pallas_call(
            functools.partial(kernel, **kw) if kw else kernel,
            out_shape=[jax.ShapeDtypeStruct(o, f32) for o in outs],
            in_specs=[vmem] * len(args),
            out_specs=[vmem] * len(outs),
            input_output_aliases=aliases,
            scratch_shapes=[pltpu.VMEM(shape, f32) for shape in scratch],
            compiler_params=pltpu.CompilerParams(vmem_limit_bytes=limit * 2**20),
        )(*args)

    sides = 1 if ny == 2 else 2
    message = (FULL1 * cols + HALF1 * cols // 2, headings)
    mid, send1, send2, *slabs = call(
        prep_kernel,
        [(rows, cols, headings), message, message] + [(rows, OFF, headings)] * sides,
        start_value.reshape(headings * rows, cols),
    )
    pairs1 = [(i, i ^ 1) for i in range(nx)]
    pairs2 = [(i, j) for i in range(nx) for j in [((i + 1) ^ 1) - 1] if 0 <= j < nx]
    if sides == 1:
        yslabs = [lax.ppermute(slabs[0], "py", [(0, 1), (1, 0)])]
    else:
        yslabs = [
            lax.ppermute(slabs[0], "py", [(i, i + 1) for i in range(ny - 1)]),
            lax.ppermute(slabs[1], "py", [(i + 1, i) for i in range(ny - 1)]),
        ]
    recv1 = lax.ppermute(send1, "px", pairs1)
    recv2 = lax.ppermute(send2, "px", pairs2)
    corners = jnp.stack(yslabs)
    even = lax.rem(lax.axis_index("px"), 2) == 0
    top = lax.slice_in_dim(corners, rows - DEPTH, rows, axis=1)
    bottom = lax.slice_in_dim(corners, 0, DEPTH, axis=1)
    side1 = lax.ppermute(jnp.where(even, top, bottom), "px", pairs1)
    side2 = lax.ppermute(jnp.where(even, bottom, top), "px", pairs2)

    tables = [stage_constants(headings, part) for part in (1.0, 0.25, 2.0 / 3.0)]
    table = jnp.asarray(np.stack([t[0] for t in tables]))
    common = dict(turns=[t[1] for t in tables], gap=gap)
    seg = columns_of(cols, 6)[0]
    wide = cols + 2 * OFF
    tall = (rows + 2 * DEPTH, wide, headings)
    short = (rows + 6, wide, headings)
    scratch = [(max(rows - 6, 12), seg, SUB, LANES)]
    field, one = call(inner_kernel, [tall, short], table, mid, yslabs[0], yslabs[-1], scratch=scratch, **common)

    blocks = call(spread_kernel, [(nx, headings // nx, rows, cols)], prior)[0]
    regrouped = lax.all_to_all(blocks, "px", split_axis=0, concat_axis=0, tiled=True)

    common = dict(common, rows=rows, cols=cols)
    count = columns_of(cols, 3)[0] * SUB
    message = (FULL2 * count + HALF2 * count // 2, headings)
    field, one, two, send1, send2 = call(
        outer_kernel, [tall, short, short, message, message],
        table, recv1, recv2, side1, side2, field, one, aliases={5: 0, 6: 1}, scratch=scratch, **common,
    )
    recv1 = lax.ppermute(send1, "px", pairs1)
    recv2 = lax.ppermute(send2, "px", pairs2)
    two, three = call(
        middle_kernel, [short, (rows, wide, headings)], table, field, one, two, aliases={3: 0}, scratch=scratch, **common
    )
    out = call(
        last_kernel, [(headings * rows, cols), short, (rows, wide, headings)],
        table, recv1, recv2, field, two, three, regrouped.reshape(headings * rows, cols), reach, avoid,
        aliases={4: 1, 5: 2}, scratch=scratch, **common,
    )[0]
    return out.reshape(headings, rows, cols)


def solution(mesh):
    return jax.shard_map(
        on_device,
        mesh=mesh,
        in_specs=(P(None, "px", "py"), P("px", None, "py"), P("px", "py"), P("px", "py")),
        out_specs=P(None, "px", "py"),
        check_vma=False,
    )
```

```python
import functools
import math

import jax
import jax.numpy as jnp
import numpy as np
from jax import lax
from jax.experimental import pallas as pl
from jax.experimental.pallas import tpu as pltpu
from jax.sharding import PartitionSpec as P


EPS = 1e-06
SPACING = 1.0 / 64.0
SPEED = 1.0
TURN = 2.0
COURANT = 0.5
LANES = 128
SUB = 8
DEPTH = 6
OFF = 16


LIMIT = 12


def ceil_div(a, b):
    return -(-a // b)


def stage_constants(headings, share):
    gap = 2.0 * math.pi / headings
    dt = COURANT / (2.0 * SPEED / SPACING + TURN / gap)
    angles = (np.float32(gap) * np.arange(headings, dtype=np.float32)).astype(np.float64)
    rows = []
    for wave in (np.cos(angles), np.sin(angles)):
        g = share * dt * SPEED * wave / SPACING
        ahead = wave >= 0
        rows += [
            g,
            np.where(ahead, -g / 3, g / 6),
            np.where(ahead, -g / 6, g / 3),
            np.where(ahead, 0.5, 1.0 / 6.0),
            np.where(ahead, 1.0 / 6.0, 0.5),
            np.where(ahead, g / 6, -g / 3),
            np.where(ahead, g / 3, -g / 6),
            np.where(ahead, 1.0, 0.0),
        ]
    turn = share * dt * TURN / (6.0 * gap)
    return np.stack(rows).astype(np.float32), float(turn)


def weights_of(a, b, d, eps, want):
    bd = b * d
    ad = a * d
    ab = a * b
    mid = (bd - ad) * (2.0 / 3.0) + (ab * 0.5 + eps)
    out = []
    for name in want:
        x = {"L": mid + bd if "L" in want else None, "C": mid, "R": mid - ad if "R" in want else None}[name]
        r = inverse(x)
        out.append(r * r)
    return out


def inverse(x):
    return 1.0 / x


def sided(vals, coef, eps):
    n = len(vals)
    g, r2, r3, n1c, n3c, k1, k3 = coef
    u = [vals[i + 1] - vals[i] for i in range(n - 1)]
    w = [None] + [u[i] - u[i - 1] for i in range(1, n - 1)]
    d = [None] + [w[i + 1] - w[i] for i in range(1, n - 2)]
    tri = [None] + [weights_of(w[i], w[i + 1], d[i], eps, "LCR") for i in range(1, n - 2)]
    third = [None, None] + [d[i] - d[i - 1] for i in range(2, n - 2)]
    faces = {}
    for k in range(2, n - 3):
        m1 = tri[k - 1][0] * n1c
        m2 = tri[k][1]
        m3 = tri[k + 1][2] * n3c
        den = (m1 + m3) + m2
        num = m1 * (k1 * third[k]) + m3 * (k3 * third[k + 1])
        smooth = g * u[k] + r2 * w[k] + r3 * w[k + 1]
        faces[k] = smooth + num * inverse(den)
    return faces


def turning(v, eps):
    ahead = lambda x: pltpu.roll(x, LANES - 1, x.ndim - 1)
    behind = lambda x: pltpu.roll(x, 1, x.ndim - 1)
    u = ahead(v) - v
    w = u - behind(u)
    wn = ahead(w)
    d = wn - w
    low, mid, high = weights_of(w, wn, d, eps, "LCR")
    m1 = behind(low)
    m3 = ahead(high)
    g1 = d - behind(d)
    g2 = ahead(g1)
    v0 = (m1 + m3) * 0.5 + mid * 3.0
    a1 = m1 * g1
    a3 = m3 * g2
    s = w + wn
    top = u * 6.0 + wn + s
    back = (a1 + 1.5 * a3) * inverse(v0 + m3) - top
    fore = (top - 3.0 * s) + (a3 + 1.5 * a1) * inverse(v0 + m1)
    return jnp.minimum(behind(back), fore)


def lanes_of(shape):
    return lax.broadcasted_iota(jnp.int32, shape, len(shape) - 1)


def fold(rows, shift):
    half = rows.shape[0] // 2
    low = pltpu.roll(rows[:half], (-shift) % LANES, 1)
    high = pltpu.roll(rows[half:], shift % LANES, 1)
    return jnp.where(lanes_of(low.shape) < LANES // 2, low, high)


def unfold(packed, shift):
    return pltpu.roll(packed, shift % LANES, 1), pltpu.roll(packed, (-shift) % LANES, 1)


QUARTER = LANES // 4
FULL1, HALF1 = 4, 2
FULL2, HALF2 = 2, 1


def even_tile():
    return lax.rem(lax.axis_index("px"), 2) == 0


def pack(ref, read, count, full, half):
    for i in range(full):
        ref[pl.ds(i * count, count), :] = read(i)[0]
    for i in range(half):
        values, shift = read(full + i)
        ref[pl.ds(full * count + i * (count // 2), count // 2), :] = fold(values, shift)


def pack_pair(one_ref, two_ref, row, rows, count, full, half):
    upper = lambda i: (row(rows - 1 - i), QUARTER)
    lower = lambda i: (row(i), -QUARTER)

    @pl.when(even_tile())
    def _():
        pack(one_ref, upper, count, full, half)
        pack(two_ref, lower, count, full, half)

    @pl.when(jnp.logical_not(even_tile()))
    def _():
        pack(one_ref, lower, count, full, half)
        pack(two_ref, upper, count, full, half)


def unpack_pair(one_ref, two_ref, write, rows, count, full, half):
    def unpack(ref, low):
        at = lambda i: -1 - i if low else rows + i
        for i in range(full):
            write(at(i), 0, ref[pl.ds(i * count, count), :])
        for i in range(half):
            packed = ref[pl.ds(full * count + i * (count // 2), count // 2), :]
            first, second = unfold(packed, QUARTER if low else -QUARTER)
            write(at(full + i), 0, first)
            write(at(full + i), count // 2, second)

    @pl.when(even_tile())
    def _():
        unpack(one_ref, False)
        unpack(two_ref, True)

    @pl.when(jnp.logical_not(even_tile()))
    def _():
        unpack(one_ref, True)
        unpack(two_ref, False)


def prep_kernel(x_ref, mid_ref, one_ref, two_ref, *slabs):
    rows, cols = mid_ref.shape[:2]
    for r in range(rows):
        mid_ref[r] = x_ref[pl.ds(r, LANES, stride=rows), :].T
    pack_pair(one_ref, two_ref, lambda r: mid_ref[r], rows, cols, FULL1, HALF1)
    right = lambda ref: ref.__setitem__(Ellipsis, mid_ref[:, pl.ds(cols - OFF, OFF), :])
    left = lambda ref: ref.__setitem__(Ellipsis, mid_ref[:, pl.ds(0, OFF), :])
    if len(slabs) == 1:
        pl.when(lax.axis_index("py") == 0)(lambda: right(slabs[0]))
        pl.when(lax.axis_index("py") != 0)(lambda: left(slabs[0]))
    else:
        right(slabs[0])
        left(slabs[1])


def spread_kernel(p_ref, after_ref, o_ref):
    del after_ref
    rows = o_ref.shape[2]
    for i in range(o_ref.shape[0]):
        o_ref[i] = p_ref[:, pl.ds(i * rows, rows), :]


def columns_of(cols, margin):
    seg = ceil_div(cols + 2 * margin, SUB)
    return seg, -((seg * SUB - cols) // 2)


def stage(index, src, dst, base, part, const_ref, parts, sizes, turn):
    cols, margin, gap = sizes
    seg, start = columns_of(cols, margin)
    eps_xy = 0.5 * EPS * SPACING**2
    eps_t = 0.5 * EPS * gap**2
    weights = (None, (0.25, 0.75), (2.0 / 3.0, 1.0 / 3.0))[index]

    def column(array, row, j):
        return array[0][row + array[1], pl.ds(OFF + start + j, SUB, stride=seg), :]

    def const(i):
        return const_ref[index, pl.ds(i, SUB, stride=0), :]

    xcoef = [const(i) for i in range(7)]
    ycoef = [const(i) for i in range(8, 15)]
    xmask = const(7) > 0.5
    ymask = const(15) > 0.5

    @pl.loop(0, seg)
    def _(j):
        at = 0
        for lo, hi in parts:
            vals = [column(src, r, j) for r in range(lo - 3, hi + 3)]
            faces = sided(vals, xcoef, eps_xy)
            for r in range(lo, hi):
                i = r - lo + 3
                move = jnp.where(xmask, faces[i], faces[i - 1])
                here = vals[i]
                if weights is not None:
                    here = here * weights[0] + column(base, r, j) * weights[1]
                part[at, j] = here + move
                at += 1

    counts = [hi - lo for lo, hi in parts]

    @pl.loop(0, sum(counts))
    def _(t):
        row = t + parts[0][0]
        if len(parts) == 2:
            row = jnp.where(t < counts[0], row, t - counts[0] + parts[1][0])
        vals = [column(src, row, j) for j in range(-3, seg + 3)]
        faces = sided(vals, ycoef, eps_xy)
        for j in range(seg):
            i = j + 3
            move = jnp.where(ymask, faces[i], faces[i - 1])
            out = part[t, j] + move + turn * turning(vals[i], eps_t)
            dst[0][row + dst[1], pl.ds(OFF + start + j, SUB, stride=seg), :] = out


def clear_columns(dst, parts, cols):
    py = lax.axis_index("py")
    for edge, begin in ((0, 0), (lax.axis_size("py") - 1, OFF + cols)):

        @pl.when(py == edge)
        def _():
            for lo, hi in parts:
                dst[0][pl.ds(lo + dst[1], hi - lo), pl.ds(begin, OFF), :] = jnp.zeros((hi - lo, OFF, LANES), jnp.float32)


def inner_kernel(const_ref, mid_ref, ylow_ref, yhigh_ref, field, one, part, *, turns, gap):
    rows, cols = mid_ref.shape[:2]
    own = pl.ds(DEPTH, rows)
    field[own, pl.ds(OFF, cols), :] = mid_ref[...]
    field[own, pl.ds(0, OFF), :] = ylow_ref[...]
    field[own, pl.ds(OFF + cols, OFF), :] = yhigh_ref[...]
    clear_columns((field, DEPTH), [(0, rows)], cols)
    parts = [(3, rows - 3)]
    stage(0, (field, DEPTH), (one, 3), None, part, const_ref, parts, (cols, 6, gap), turns[0])
    clear_columns((one, 3), parts, cols)


def outer_kernel(const_ref, recv1_ref, recv2_ref, side1_ref, side2_ref, field_in, one_in, field, one, two, send1, send2, part, *, turns, gap, rows, cols):
    del field_in, one_in

    def write(row, col, values):
        field[row + DEPTH, pl.ds(OFF + col, values.shape[0]), :] = values

    unpack_pair(recv1_ref, recv2_ref, write, rows, cols, FULL1, HALF1)
    low, high = pl.ds(0, DEPTH), pl.ds(DEPTH + rows, DEPTH)

    def sides(ref, where):
        field[where, pl.ds(0, OFF), :] = ref[0]
        field[where, pl.ds(OFF + cols, OFF), :] = ref[ref.shape[0] - 1]

    @pl.when(even_tile())
    def _():
        sides(side1_ref, high)
        sides(side2_ref, low)

    @pl.when(jnp.logical_not(even_tile()))
    def _():
        sides(side1_ref, low)
        sides(side2_ref, high)

    clear_columns((field, DEPTH), [(-DEPTH, 0), (rows, rows + DEPTH)], cols)
    parts = [(-3, 3), (rows - 3, rows + 3)]
    stage(0, (field, DEPTH), (one, 3), None, part, const_ref, parts, (cols, 6, gap), turns[0])
    clear_columns((one, 3), parts, cols)
    px = lax.axis_index("px")
    for edge, begin in ((0, 0), (lax.axis_size("px") - 1, 3 + rows)):

        @pl.when(px == edge)
        def _():
            one[pl.ds(begin, 3)] = jnp.zeros((3,) + one.shape[1:], jnp.float32)

    parts = [(0, 3), (rows - 3, rows)]
    stage(1, (one, 3), (two, 3), (field, DEPTH), part, const_ref, parts, (cols, 3, gap), turns[1])
    clear_columns((two, 3), parts, cols)
    seg, start = columns_of(cols, 3)
    count = seg * SUB
    pack_pair(send1, send2, lambda r: two[r + 3, pl.ds(OFF + start, count), :], rows, count, FULL2, HALF2)


def middle_kernel(const_ref, field, one, two_in, two, three, part, *, turns, gap, rows, cols):
    del two_in
    parts = [(3, rows - 3)]
    stage(1, (one, 3), (two, 3), (field, DEPTH), part, const_ref, parts, (cols, 3, gap), turns[1])
    clear_columns((two, 3), parts, cols)
    stage(2, (two, 3), (three, 0), (field, DEPTH), part, const_ref, parts, (cols, 0, gap), turns[2])


def last_kernel(const_ref, recv1_ref, recv2_ref, field, two_in, three_in, o_ref, two, three, part, *, turns, gap, rows, cols):
    del two_in, three_in
    seg, start = columns_of(cols, 3)

    def write(row, col, values):
        two[row + 3, pl.ds(OFF + start + col, values.shape[0]), :] = values

    unpack_pair(recv1_ref, recv2_ref, write, rows, seg * SUB, FULL2, HALF2)
    parts = [(0, 3), (rows - 3, rows)]
    stage(2, (two, 3), (three, 0), (field, DEPTH), part, const_ref, parts, (cols, 0, gap), turns[2])
    for r in range(rows):
        o_ref[pl.ds(r, LANES, stride=rows), :] = three[r, pl.ds(OFF, cols), :].T


def on_device(start_value, prior, reach, avoid):
    headings, rows, cols = start_value.shape
    nx, ny = lax.axis_size("px"), lax.axis_size("py")
    assert headings == LANES and cols == LANES and rows >= 2 * DEPTH and nx % 2 == 0
    gap = 2.0 * math.pi / headings
    f32 = jnp.float32
    vmem = pl.BlockSpec(memory_space=pltpu.VMEM)

    def call(kernel, outs, *args, limit=LIMIT, aliases={}, scratch=(), untouched=(), **kw):
        return pl.pallas_call(
            functools.partial(kernel, **kw) if kw else kernel,
            out_shape=[jax.ShapeDtypeStruct(o, f32) for o in outs],
            in_specs=[pl.BlockSpec(memory_space=pl.ANY) if i in untouched else vmem for i in range(len(args))],
            out_specs=[vmem] * len(outs),
            input_output_aliases=aliases,
            scratch_shapes=[pltpu.VMEM(shape, f32) for shape in scratch],
            compiler_params=pltpu.CompilerParams(vmem_limit_bytes=limit * 2**20),
        )(*args)

    sides = 1 if ny == 2 else 2
    message = (FULL1 * cols + HALF1 * cols // 2, headings)
    mid, send1, send2, *slabs = call(
        prep_kernel,
        [(rows, cols, headings), message, message] + [(rows, OFF, headings)] * sides,
        start_value.reshape(headings * rows, cols),
    )
    pairs1 = [(i, i ^ 1) for i in range(nx)]
    pairs2 = [(i, j) for i in range(nx) for j in [((i + 1) ^ 1) - 1] if 0 <= j < nx]
    if sides == 1:
        yslabs = [lax.ppermute(slabs[0], "py", [(0, 1), (1, 0)])]
    else:
        yslabs = [
            lax.ppermute(slabs[0], "py", [(i, i + 1) for i in range(ny - 1)]),
            lax.ppermute(slabs[1], "py", [(i + 1, i) for i in range(ny - 1)]),
        ]
    recv1 = lax.ppermute(send1, "px", pairs1)
    recv2 = lax.ppermute(send2, "px", pairs2)
    corners = jnp.stack(yslabs)
    even = lax.rem(lax.axis_index("px"), 2) == 0
    top = lax.slice_in_dim(corners, rows - DEPTH, rows, axis=1)
    bottom = lax.slice_in_dim(corners, 0, DEPTH, axis=1)
    side1 = lax.ppermute(jnp.where(even, top, bottom), "px", pairs1)
    side2 = lax.ppermute(jnp.where(even, bottom, top), "px", pairs2)

    tables = [stage_constants(headings, part) for part in (1.0, 0.25, 2.0 / 3.0)]
    table = jnp.asarray(np.stack([t[0] for t in tables]))
    common = dict(turns=[t[1] for t in tables], gap=gap)
    seg = columns_of(cols, 6)[0]
    wide = cols + 2 * OFF
    tall = (rows + 2 * DEPTH, wide, headings)
    short = (rows + 6, wide, headings)
    scratch = [(max(rows - 6, 12), seg, SUB, LANES)]
    field, one = call(inner_kernel, [tall, short], table, mid, yslabs[0], yslabs[-1], scratch=scratch, **common)

    blocks = call(spread_kernel, [(nx, headings // nx, rows, cols)], prior, one, untouched=(1,))[0]
    regrouped = lax.all_to_all(blocks, "px", split_axis=0, concat_axis=0, tiled=True)

    common = dict(common, rows=rows, cols=cols)
    count = columns_of(cols, 3)[0] * SUB
    message = (FULL2 * count + HALF2 * count // 2, headings)
    field, one, two, send1, send2 = call(
        outer_kernel, [tall, short, short, message, message],
        table, recv1, recv2, side1, side2, field, one, aliases={5: 0, 6: 1}, scratch=scratch, **common,
    )
    recv1 = lax.ppermute(send1, "px", pairs1)
    recv2 = lax.ppermute(send2, "px", pairs2)
    two, three = call(
        middle_kernel, [short, (rows, wide, headings)], table, field, one, two, aliases={3: 0}, scratch=scratch, **common
    )
    third = call(
        last_kernel, [(headings * rows, cols), short, (rows, wide, headings)],
        table, recv1, recv2, field, two, three,
        aliases={4: 1, 5: 2}, scratch=scratch, **common,
    )[0]
    third = third.reshape(headings, rows, cols)
    return jnp.minimum(regrouped.reshape(headings, rows, cols), jnp.maximum(avoid[None], jnp.minimum(reach[None], third)))


def solution(mesh):
    return jax.shard_map(
        on_device,
        mesh=mesh,
        in_specs=(P(None, "px", "py"), P("px", None, "py"), P("px", "py"), P("px", "py")),
        out_specs=P(None, "px", "py"),
        check_vma=False,
    )
```

```python
import functools
import math

import jax
import jax.numpy as jnp
import numpy as np
from jax import lax
from jax.experimental import pallas as pl
from jax.experimental.pallas import tpu as pltpu
from jax.sharding import PartitionSpec as P


EPS = 1e-06
SPACING = 1.0 / 64.0
SPEED = 1.0
TURN = 2.0
COURANT = 0.5
LANES = 128
SUB = 8
DEPTH = 6
OFF = 16


LIMIT = 12


def ceil_div(a, b):
    return -(-a // b)


def stage_constants(headings, share):
    gap = 2.0 * math.pi / headings
    dt = COURANT / (2.0 * SPEED / SPACING + TURN / gap)
    angles = (np.float32(gap) * np.arange(headings, dtype=np.float32)).astype(np.float64)
    rows = []
    for wave in (np.cos(angles), np.sin(angles)):
        g = share * dt * SPEED * wave / SPACING
        ahead = wave >= 0
        rows += [
            g,
            np.where(ahead, -g / 3, g / 6),
            np.where(ahead, -g / 6, g / 3),
            np.where(ahead, 0.5, 1.0 / 6.0),
            np.where(ahead, 1.0 / 6.0, 0.5),
            np.where(ahead, g / 6, -g / 3),
            np.where(ahead, g / 3, -g / 6),
            np.where(ahead, 1.0, 0.0),
        ]
    turn = share * dt * TURN / (6.0 * gap)
    return np.stack(rows).astype(np.float32), float(turn)


def weights_of(a, b, d, eps, want):
    bd = b * d
    ad = a * d
    ab = a * b
    mid = (bd - ad) * (2.0 / 3.0) + (ab * 0.5 + eps)
    out = []
    for name in want:
        x = {"L": mid + bd if "L" in want else None, "C": mid, "R": mid - ad if "R" in want else None}[name]
        r = inverse(x)
        out.append(r * r)
    return out


def inverse(x):
    return 1.0 / x


def sided(vals, coef, eps):
    n = len(vals)
    g, r2, r3, n1c, n3c, k1, k3 = coef
    u = [vals[i + 1] - vals[i] for i in range(n - 1)]
    w = [None] + [u[i] - u[i - 1] for i in range(1, n - 1)]
    d = [None] + [w[i + 1] - w[i] for i in range(1, n - 2)]
    tri = [None] + [weights_of(w[i], w[i + 1], d[i], eps, "LCR") for i in range(1, n - 2)]
    third = [None, None] + [d[i] - d[i - 1] for i in range(2, n - 2)]
    faces = {}
    for k in range(2, n - 3):
        m1 = tri[k - 1][0] * n1c
        m2 = tri[k][1]
        m3 = tri[k + 1][2] * n3c
        den = (m1 + m3) + m2
        num = m1 * (k1 * third[k]) + m3 * (k3 * third[k + 1])
        smooth = g * u[k] + r2 * w[k] + r3 * w[k + 1]
        faces[k] = smooth + num * inverse(den)
    return faces


def turning(v, eps):
    ahead = lambda x: pltpu.roll(x, LANES - 1, x.ndim - 1)
    behind = lambda x: pltpu.roll(x, 1, x.ndim - 1)
    u = ahead(v) - v
    w = u - behind(u)
    wn = ahead(w)
    d = wn - w
    low, mid, high = weights_of(w, wn, d, eps, "LCR")
    m1 = behind(low)
    m3 = ahead(high)
    g1 = d - behind(d)
    g2 = ahead(g1)
    v0 = (m1 + m3) * 0.5 + mid * 3.0
    a1 = m1 * g1
    a3 = m3 * g2
    s = w + wn
    top = u * 6.0 + wn + s
    back = (a1 + 1.5 * a3) * inverse(v0 + m3) - top
    fore = (top - 3.0 * s) + (a3 + 1.5 * a1) * inverse(v0 + m1)
    return jnp.minimum(behind(back), fore)


def lanes_of(shape):
    return lax.broadcasted_iota(jnp.int32, shape, len(shape) - 1)


def fold(rows, shift):
    half = rows.shape[0] // 2
    low = pltpu.roll(rows[:half], (-shift) % LANES, 1)
    high = pltpu.roll(rows[half:], shift % LANES, 1)
    return jnp.where(lanes_of(low.shape) < LANES // 2, low, high)


def unfold(packed, shift):
    return pltpu.roll(packed, shift % LANES, 1), pltpu.roll(packed, (-shift) % LANES, 1)


QUARTER = LANES // 4
FULL1, HALF1 = 4, 2
FULL2, HALF2 = 2, 1


def even_tile():
    return lax.rem(lax.axis_index("px"), 2) == 0


def pack(ref, read, count, full, half):
    for i in range(full):
        ref[pl.ds(i * count, count), :] = read(i)[0]
    for i in range(half):
        values, shift = read(full + i)
        ref[pl.ds(full * count + i * (count // 2), count // 2), :] = fold(values, shift)


def pack_pair(one_ref, two_ref, row, rows, count, full, half):
    upper = lambda i: (row(rows - 1 - i), QUARTER)
    lower = lambda i: (row(i), -QUARTER)

    @pl.when(even_tile())
    def _():
        pack(one_ref, upper, count, full, half)
        pack(two_ref, lower, count, full, half)

    @pl.when(jnp.logical_not(even_tile()))
    def _():
        pack(one_ref, lower, count, full, half)
        pack(two_ref, upper, count, full, half)


def unpack_pair(one_ref, two_ref, write, rows, count, full, half):
    def unpack(ref, low):
        at = lambda i: -1 - i if low else rows + i
        for i in range(full):
            write(at(i), 0, ref[pl.ds(i * count, count), :])
        for i in range(half):
            packed = ref[pl.ds(full * count + i * (count // 2), count // 2), :]
            first, second = unfold(packed, QUARTER if low else -QUARTER)
            write(at(full + i), 0, first)
            write(at(full + i), count // 2, second)

    @pl.when(even_tile())
    def _():
        unpack(one_ref, False)
        unpack(two_ref, True)

    @pl.when(jnp.logical_not(even_tile()))
    def _():
        unpack(one_ref, True)
        unpack(two_ref, False)


def prep_kernel(x_ref, const_ref, own_ref, *slabs):
    del const_ref
    rows = own_ref.shape[0]
    cols = x_ref.shape[1]
    for r in range(rows):
        own_ref[r, pl.ds(OFF, cols), :] = x_ref[pl.ds(r, LANES, stride=rows), :].T

    def cut(ref, begin):
        ref[...] = own_ref[:, pl.ds(begin, OFF), :]

    if len(slabs) == 1:
        pl.when(lax.axis_index("py") == 0)(lambda: cut(slabs[0], cols))
        pl.when(lax.axis_index("py") != 0)(lambda: cut(slabs[0], OFF))
    else:
        cut(slabs[0], cols)
        cut(slabs[1], OFF)


def send_kernel(own_in, ylow_ref, yhigh_ref, own, one_ref, two_ref):
    del own_in
    rows, wide = own.shape[:2]
    cols = wide - 2 * OFF
    own[:, pl.ds(0, OFF), :] = ylow_ref[...]
    own[:, pl.ds(OFF + cols, OFF), :] = yhigh_ref[...]
    clear_columns((own, 0), [(0, rows)], cols)
    for begin, count, at in message_parts(cols):
        read = lambda r: own[r, pl.ds(beside(begin), count), :]
        where = pl.ds(at, message_lines(count))
        pack_pair(one_ref.at[where], two_ref.at[where], read, rows, count, FULL1, HALF1)


def message_parts(cols):
    begins = [0, -OFF, cols]
    if lax.axis_size("py") == 2:
        begins = [0, pl.multiple_of(jnp.where(lax.axis_index("py") == 0, cols, -OFF), OFF)]
    parts, at = [], 0
    for begin in begins:
        count = OFF if parts else cols
        parts.append((begin, count, at))
        at += message_lines(count)
    return parts


def beside(begin):
    return OFF + begin if isinstance(begin, int) else pl.multiple_of(OFF + begin, OFF)


def message_lines(count):
    return FULL1 * count + HALF1 * (count // 2)


def spread_kernel(p_ref, after_ref, o_ref, held, came, gone):
    del after_ref
    count, rows = o_ref.shape[0], o_ref.shape[2]
    load = lambda i: pltpu.make_async_copy(p_ref.at[:, pl.ds(i * rows, rows), :], held.at[i], came.at[i])
    save = lambda i: pltpu.make_async_copy(held.at[i], o_ref.at[i], gone.at[i])
    for i in range(count):
        load(i).start()
    for i in range(count):
        load(i).wait()
        save(i).start()
    for i in range(count):
        save(i).wait()


def columns_of(cols, margin):
    seg = ceil_div(cols + 2 * margin, SUB)
    return seg, -((seg * SUB - cols) // 2)


def stage(index, src, dst, base, part, const_ref, parts, sizes, turn):
    cols, margin, gap = sizes
    seg, start = columns_of(cols, margin)
    eps_xy = 0.5 * EPS * SPACING**2
    eps_t = 0.5 * EPS * gap**2
    weights = (None, (0.25, 0.75), (2.0 / 3.0, 1.0 / 3.0))[index]

    def column(array, row, j):
        return array[0][row + array[1], pl.ds(OFF + start + j, SUB, stride=seg), :]

    def const(i):
        return const_ref[index, pl.ds(i, SUB, stride=0), :]

    xcoef = [const(i) for i in range(7)]
    ycoef = [const(i) for i in range(8, 15)]
    xmask = const(7) > 0.5
    ymask = const(15) > 0.5

    @pl.loop(0, seg)
    def _(j):
        at = 0
        for lo, hi in parts:
            vals = [column(src, r, j) for r in range(lo - 3, hi + 3)]
            faces = sided(vals, xcoef, eps_xy)
            for r in range(lo, hi):
                i = r - lo + 3
                move = jnp.where(xmask, faces[i], faces[i - 1])
                here = vals[i]
                if weights is not None:
                    here = here * weights[0] + column(base, r, j) * weights[1]
                part[at, j] = here + move
                at += 1

    counts = [hi - lo for lo, hi in parts]

    @pl.loop(0, sum(counts))
    def _(t):
        row = t + parts[0][0]
        if len(parts) == 2:
            row = jnp.where(t < counts[0], row, t - counts[0] + parts[1][0])
        vals = [column(src, row, j) for j in range(-3, seg + 3)]
        faces = sided(vals, ycoef, eps_xy)
        for j in range(seg):
            i = j + 3
            move = jnp.where(ymask, faces[i], faces[i - 1])
            out = part[t, j] + move + turn * turning(vals[i], eps_t)
            dst[0][row + dst[1], pl.ds(OFF + start + j, SUB, stride=seg), :] = out


def clear_columns(dst, parts, cols):
    py = lax.axis_index("py")
    for edge, begin in ((0, 0), (lax.axis_size("py") - 1, OFF + cols)):

        @pl.when(py == edge)
        def _():
            for lo, hi in parts:
                dst[0][pl.ds(lo + dst[1], hi - lo), pl.ds(begin, OFF), :] = jnp.zeros((hi - lo, OFF, LANES), jnp.float32)


def inner_kernel(const_ref, own, one, part, *, turns, gap):
    rows, wide = own.shape[:2]
    cols = wide - 2 * OFF
    parts = [(3, rows - 3)]
    stage(0, (own, 0), (one, -3), None, part, const_ref, parts, (cols, 6, gap), turns[0])
    clear_columns((one, -3), parts, cols)


def outer_kernel(const_ref, recv1_ref, recv2_ref, own, inner, one, two, send1, send2, field, part, *, turns, gap):
    rows, wide = own.shape[:2]
    cols = wide - 2 * OFF

    def write(row, col, values):
        field[row + DEPTH, pl.ds(beside(begin) + col, values.shape[0]), :] = values

    for begin, count, at in message_parts(cols):
        where = pl.ds(at, message_lines(count))
        unpack_pair(recv1_ref.at[where], recv2_ref.at[where], write, rows, count, FULL1, HALF1)
    clear_columns((field, DEPTH), [(-DEPTH, 0), (rows, rows + DEPTH)], cols)
    field[pl.ds(DEPTH, DEPTH)] = own[pl.ds(0, DEPTH)]
    field[pl.ds(rows, DEPTH)] = own[pl.ds(rows - DEPTH, DEPTH)]
    one[pl.ds(6, rows - 6)] = inner[...]
    parts = [(-3, 3), (rows - 3, rows + 3)]
    stage(0, (field, DEPTH), (one, 3), None, part, const_ref, parts, (cols, 6, gap), turns[0])
    clear_columns((one, 3), parts, cols)
    px = lax.axis_index("px")
    for edge, begin in ((0, 0), (lax.axis_size("px") - 1, 3 + rows)):

        @pl.when(px == edge)
        def _():
            one[pl.ds(begin, 3)] = jnp.zeros((3,) + one.shape[1:], jnp.float32)

    parts = [(0, 3), (rows - 3, rows)]
    stage(1, (one, 3), (two, 3), (own, 0), part, const_ref, parts, (cols, 3, gap), turns[1])
    clear_columns((two, 3), parts, cols)
    seg, start = columns_of(cols, 3)
    count = seg * SUB
    pack_pair(send1, send2, lambda r: two[r + 3, pl.ds(OFF + start, count), :], rows, count, FULL2, HALF2)


def middle_kernel(const_ref, own, one, two_in, two, three, part, *, turns, gap):
    del two_in
    rows, wide = own.shape[:2]
    cols = wide - 2 * OFF
    parts = [(3, rows - 3)]
    stage(1, (one, 3), (two, 3), (own, 0), part, const_ref, parts, (cols, 3, gap), turns[1])
    clear_columns((two, 3), parts, cols)
    stage(2, (two, 3), (three, 0), (own, 0), part, const_ref, parts, (cols, 0, gap), turns[2])


def last_kernel(const_ref, recv1_ref, recv2_ref, own, two_in, three_in, o_ref, two, three, part, *, turns, gap):
    del two_in, three_in
    rows, wide = own.shape[:2]
    cols = wide - 2 * OFF
    seg, start = columns_of(cols, 3)

    def write(row, col, values):
        two[row + 3, pl.ds(OFF + start + col, values.shape[0]), :] = values

    unpack_pair(recv1_ref, recv2_ref, write, rows, seg * SUB, FULL2, HALF2)
    parts = [(0, 3), (rows - 3, rows)]
    stage(2, (two, 3), (three, 0), (own, 0), part, const_ref, parts, (cols, 0, gap), turns[2])
    for r in range(rows):
        o_ref[pl.ds(r, LANES, stride=rows), :] = three[r, pl.ds(OFF, cols), :].T


def final_kernel(third_ref, prior_ref, reach_ref, avoid_ref, o_ref):
    kept = jnp.maximum(avoid_ref[...][None], jnp.minimum(reach_ref[...][None], third_ref[...]))
    o_ref[...] = jnp.minimum(prior_ref[...], kept)


def on_device(start_value, prior, reach, avoid):
    headings, rows, cols = start_value.shape
    nx, ny = lax.axis_size("px"), lax.axis_size("py")
    assert headings == LANES and cols == LANES and rows >= 2 * DEPTH and nx % 2 == 0
    gap = 2.0 * math.pi / headings
    f32 = jnp.float32
    vmem = pl.BlockSpec(memory_space=pltpu.VMEM)

    def call(kernel, outs, *args, limit=LIMIT, aliases={}, scratch=(), **kw):
        return pl.pallas_call(
            functools.partial(kernel, **kw) if kw else kernel,
            out_shape=[jax.ShapeDtypeStruct(o, f32) for o in outs],
            in_specs=[vmem] * len(args),
            out_specs=[vmem] * len(outs),
            input_output_aliases=aliases,
            scratch_shapes=[pltpu.VMEM(shape, f32) for shape in scratch],
            compiler_params=pltpu.CompilerParams(vmem_limit_bytes=limit * 2**20),
        )(*args)

    tables = [stage_constants(headings, part) for part in (1.0, 0.25, 2.0 / 3.0)]
    table = jnp.asarray(np.stack([t[0] for t in tables]))
    common = dict(turns=[t[1] for t in tables], gap=gap)
    seg = columns_of(cols, 6)[0]
    wide = cols + 2 * OFF
    tall = (rows + 2 * DEPTH, wide, headings)
    short = (rows + 6, wide, headings)
    work = (max(rows - 6, 12), seg, SUB, LANES)

    sides = 1 if ny == 2 else 2
    own, *slabs = call(
        prep_kernel,
        [(rows, wide, headings)] + [(rows, OFF, headings)] * sides,
        start_value.reshape(headings * rows, cols), table,
    )
    pairs1 = [(i, i ^ 1) for i in range(nx)]
    pairs2 = [(i, j) for i in range(nx) for j in [((i + 1) ^ 1) - 1] if 0 <= j < nx]
    if sides == 1:
        yslabs = [lax.ppermute(slabs[0], "py", [(0, 1), (1, 0)])]
    else:
        yslabs = [
            lax.ppermute(slabs[0], "py", [(i, i + 1) for i in range(ny - 1)]),
            lax.ppermute(slabs[1], "py", [(i + 1, i) for i in range(ny - 1)]),
        ]
    lines = message_lines(cols) + sides * message_lines(OFF)
    own, send1, send2 = call(
        send_kernel, [(rows, wide, headings)] + [(lines, headings)] * 2, own, yslabs[0], yslabs[-1], aliases={0: 0}
    )
    recv1 = lax.ppermute(send1, "px", pairs1)
    recv2 = lax.ppermute(send2, "px", pairs2)
    inner = call(inner_kernel, [(rows - 6, wide, headings)], table, own, scratch=[work], **common)[0]

    blocks = (nx, headings // nx, rows, cols)
    hbm = pl.BlockSpec(memory_space=pltpu.HBM)
    blocks = pl.pallas_call(
        spread_kernel,
        out_shape=jax.ShapeDtypeStruct(blocks, f32),
        in_specs=[hbm, pl.BlockSpec(memory_space=pl.ANY)],
        out_specs=hbm,
        scratch_shapes=[pltpu.VMEM(blocks, f32), pltpu.SemaphoreType.DMA((nx,)), pltpu.SemaphoreType.DMA((nx,))],
        compiler_params=pltpu.CompilerParams(vmem_limit_bytes=61 * 2**20),
    )(prior, inner)
    regrouped = lax.all_to_all(blocks, "px", split_axis=0, concat_axis=0, tiled=True)

    count = columns_of(cols, 3)[0] * SUB
    message = (FULL2 * count + HALF2 * count // 2, headings)
    one, two, send1, send2 = call(
        outer_kernel, [short, short, message, message], table, recv1, recv2, own, inner, scratch=[tall, work], **common
    )
    recv1 = lax.ppermute(send1, "px", pairs1)
    recv2 = lax.ppermute(send2, "px", pairs2)
    two, three = call(
        middle_kernel, [short, (rows, wide, headings)], table, own, one, two, aliases={3: 0}, scratch=[work], **common
    )
    third = call(
        last_kernel, [(headings * rows, cols), short, (rows, wide, headings)],
        table, recv1, recv2, own, two, three, aliases={4: 1, 5: 2}, scratch=[work], **common,
    )[0]
    cut = 16
    block = pl.BlockSpec((cut, rows, cols), lambda i: (i, 0, 0))
    plane = pl.BlockSpec((rows, cols), lambda i: (0, 0))
    return pl.pallas_call(
        final_kernel,
        grid=(headings // cut,),
        out_shape=jax.ShapeDtypeStruct((headings, rows, cols), f32),
        in_specs=[block, block, plane, plane],
        out_specs=block,
        compiler_params=pltpu.CompilerParams(vmem_limit_bytes=LIMIT * 2**20),
    )(third.reshape(headings, rows, cols), regrouped.reshape(headings, rows, cols), reach, avoid)


def solution(mesh):
    return jax.shard_map(
        on_device,
        mesh=mesh,
        in_specs=(P(None, "px", "py"), P("px", None, "py"), P("px", "py"), P("px", "py")),
        out_specs=P(None, "px", "py"),
        check_vma=False,
    )
```

```python
import functools
import math

import jax
import jax.numpy as jnp
import numpy as np
from jax import lax
from jax.experimental import pallas as pl
from jax.experimental.pallas import tpu as pltpu
from jax.sharding import PartitionSpec as P


EPS = 1e-06
SPACING = 1.0 / 64.0
SPEED = 1.0
TURN = 2.0
COURANT = 0.5
SHARES = (1.0, 0.25, 2.0 / 3.0)
LANES = 128
SUB = 8
DEPTH = 6
OFF = 16


LIMIT = 12


def ceil_div(a, b):
    return -(-a // b)


def time_step(gap):
    return COURANT / (2.0 * SPEED / SPACING + TURN / gap)


def weights_of(a, b, d, eps, want):
    bd = b * d
    ad = a * d
    ab = a * b
    mid = (bd - ad) * (2.0 / 3.0) + (ab * 0.5 + eps)
    out = []
    for name in want:
        x = {"L": mid + bd if "L" in want else None, "C": mid, "R": mid - ad if "R" in want else None}[name]
        r = inverse(x)
        out.append(r * r)
    return out


def inverse(x):
    return 1.0 / x


def sided(vals, coef, eps):
    n = len(vals)
    g, r2, r3, n1c, n3c, k1, k3 = coef
    u = [vals[i + 1] - vals[i] for i in range(n - 1)]
    w = [None] + [u[i] - u[i - 1] for i in range(1, n - 1)]
    d = [None] + [w[i + 1] - w[i] for i in range(1, n - 2)]
    tri = [None] + [weights_of(w[i], w[i + 1], d[i], eps, "LCR") for i in range(1, n - 2)]
    third = [None, None] + [d[i] - d[i - 1] for i in range(2, n - 2)]
    faces = {}
    for k in range(2, n - 3):
        m1 = tri[k - 1][0] * n1c
        m2 = tri[k][1]
        m3 = tri[k + 1][2] * n3c
        den = (m1 + m3) + m2
        num = m1 * (k1 * third[k]) + m3 * (k3 * third[k + 1])
        smooth = g * u[k] + r2 * w[k] + r3 * w[k + 1]
        faces[k] = smooth + num * inverse(den)
    return faces


def turning(v, eps):
    ahead = lambda x: pltpu.roll(x, LANES - 1, x.ndim - 1)
    behind = lambda x: pltpu.roll(x, 1, x.ndim - 1)
    u = ahead(v) - v
    w = u - behind(u)
    wn = ahead(w)
    d = wn - w
    low, mid, high = weights_of(w, wn, d, eps, "LCR")
    m1 = behind(low)
    m3 = ahead(high)
    g1 = d - behind(d)
    g2 = ahead(g1)
    v0 = (m1 + m3) * 0.5 + mid * 3.0
    a1 = m1 * g1
    a3 = m3 * g2
    s = w + wn
    top = u * 6.0 + wn + s
    back = (a1 + 1.5 * a3) * inverse(v0 + m3) - top
    fore = (top - 3.0 * s) + (a3 + 1.5 * a1) * inverse(v0 + m1)
    return jnp.minimum(behind(back), fore)


def lanes_of(shape):
    return lax.broadcasted_iota(jnp.int32, shape, len(shape) - 1)


def fold(rows, shift):
    half = rows.shape[0] // 2
    low = pltpu.roll(rows[:half], (-shift) % LANES, 1)
    high = pltpu.roll(rows[half:], shift % LANES, 1)
    return jnp.where(lanes_of(low.shape) < LANES // 2, low, high)


def unfold(packed, shift):
    return pltpu.roll(packed, shift % LANES, 1), pltpu.roll(packed, (-shift) % LANES, 1)


QUARTER = LANES // 4
FULL1, HALF1 = 4, 2
FULL2, HALF2 = 2, 1


def even_tile():
    return lax.rem(lax.axis_index("px"), 2) == 0


def pack(ref, read, count, full, half):
    for i in range(full):
        ref[pl.ds(i * count, count), :] = read(i)[0]
    for i in range(half):
        values, shift = read(full + i)
        ref[pl.ds(full * count + i * (count // 2), count // 2), :] = fold(values, shift)


def pack_pair(one_ref, two_ref, row, rows, count, full, half):
    upper = lambda i: (row(rows - 1 - i), QUARTER)
    lower = lambda i: (row(i), -QUARTER)

    @pl.when(even_tile())
    def _():
        pack(one_ref, upper, count, full, half)
        pack(two_ref, lower, count, full, half)

    @pl.when(jnp.logical_not(even_tile()))
    def _():
        pack(one_ref, lower, count, full, half)
        pack(two_ref, upper, count, full, half)


def unpack_pair(one_ref, two_ref, write, rows, count, full, half):
    def unpack(ref, low):
        at = lambda i: -1 - i if low else rows + i
        for i in range(full):
            write(at(i), 0, ref[pl.ds(i * count, count), :])
        for i in range(half):
            packed = ref[pl.ds(full * count + i * (count // 2), count // 2), :]
            first, second = unfold(packed, QUARTER if low else -QUARTER)
            write(at(full + i), 0, first)
            write(at(full + i), count // 2, second)

    @pl.when(even_tile())
    def _():
        unpack(one_ref, False)
        unpack(two_ref, True)

    @pl.when(jnp.logical_not(even_tile()))
    def _():
        unpack(one_ref, True)
        unpack(two_ref, False)


def fill_table(table_ref):
    headings = table_ref.shape[2]
    gap = 2.0 * math.pi / headings
    lane = lax.broadcasted_iota(jnp.int32, (SUB, headings), 1)
    angle = lane.astype(jnp.float32) * np.float32(gap)
    behind_x = (lane >= headings // 4) & (lane < 3 * headings // 4)
    for stage_index, share in enumerate(SHARES):
        step = share * time_step(gap) * SPEED / SPACING
        for at, wave, back in ((0, jnp.cos(angle), behind_x), (8, jnp.sin(angle), lane > headings // 2)):
            g = wave * np.float32(step)
            rows = [
                g,
                g * jnp.where(back, 1.0 / 6.0, -1.0 / 3.0),
                g * jnp.where(back, 1.0 / 3.0, -1.0 / 6.0),
                jnp.where(back, 1.0 / 6.0, 0.5),
                jnp.where(back, 0.5, 1.0 / 6.0),
                g * jnp.where(back, -1.0 / 3.0, 1.0 / 6.0),
                g * jnp.where(back, -1.0 / 6.0, 1.0 / 3.0),
                jnp.where(back, 0.0, 1.0),
            ]
            for i, values in enumerate(rows):
                table_ref[stage_index, pl.ds(at + i, 1), :] = values[:1]


def prep_kernel(x_ref, own_ref, table_ref, *slabs):
    rows = own_ref.shape[0]
    cols = x_ref.shape[1]
    fill_table(table_ref)
    for r in range(rows):
        own_ref[r, pl.ds(OFF, cols), :] = x_ref[pl.ds(r, LANES, stride=rows), :].T

    def cut(ref, begin):
        ref[...] = own_ref[:, pl.ds(begin, OFF), :]

    if len(slabs) == 1:
        pl.when(lax.axis_index("py") == 0)(lambda: cut(slabs[0], cols))
        pl.when(lax.axis_index("py") != 0)(lambda: cut(slabs[0], OFF))
    else:
        cut(slabs[0], cols)
        cut(slabs[1], OFF)


def spread_kernel(p_ref, o_ref):
    rows = o_ref.shape[2]
    for i in range(o_ref.shape[0]):
        o_ref[i] = p_ref[:, pl.ds(i * rows, rows), :]


def send_kernel(own_in, ylow_ref, yhigh_ref, own, one_ref, two_ref):
    del own_in
    rows, wide = own.shape[:2]
    cols = wide - 2 * OFF
    own[:, pl.ds(0, OFF), :] = ylow_ref[...]
    own[:, pl.ds(OFF + cols, OFF), :] = yhigh_ref[...]
    clear_columns((own, 0), [(0, rows)], cols)
    for begin, count, at in message_parts(cols):
        read = lambda r: own[r, pl.ds(beside(begin), count), :]
        where = pl.ds(at, message_lines(count))
        pack_pair(one_ref.at[where], two_ref.at[where], read, rows, count, FULL1, HALF1)


def message_parts(cols):
    begins = [0, -OFF, cols]
    if lax.axis_size("py") == 2:
        begins = [0, pl.multiple_of(jnp.where(lax.axis_index("py") == 0, cols, -OFF), OFF)]
    parts, at = [], 0
    for begin in begins:
        count = OFF if parts else cols
        parts.append((begin, count, at))
        at += message_lines(count)
    return parts


def beside(begin):
    return OFF + begin if isinstance(begin, int) else pl.multiple_of(OFF + begin, OFF)


def message_lines(count):
    return FULL1 * count + HALF1 * (count // 2)


def columns_of(cols, margin):
    seg = ceil_div(cols + 2 * margin, SUB)
    return seg, -((seg * SUB - cols) // 2)


def stage(index, src, dst, base, part, const_ref, parts, sizes, turn):
    cols, margin, gap = sizes
    seg, start = columns_of(cols, margin)
    eps_xy = 0.5 * EPS * SPACING**2
    eps_t = 0.5 * EPS * gap**2
    weights = (None, (0.25, 0.75), (2.0 / 3.0, 1.0 / 3.0))[index]

    def column(array, row, j):
        return array[0][row + array[1], pl.ds(OFF + start + j, SUB, stride=seg), :]

    def const(i):
        return const_ref[index, pl.ds(i, SUB, stride=0), :]

    xcoef = [const(i) for i in range(7)]
    ycoef = [const(i) for i in range(8, 15)]
    xmask = const(7) > 0.5
    ymask = const(15) > 0.5

    @pl.loop(0, seg)
    def _(j):
        at = 0
        for lo, hi in parts:
            vals = [column(src, r, j) for r in range(lo - 3, hi + 3)]
            faces = sided(vals, xcoef, eps_xy)
            for r in range(lo, hi):
                i = r - lo + 3
                move = jnp.where(xmask, faces[i], faces[i - 1])
                here = vals[i]
                if weights is not None:
                    here = here * weights[0] + column(base, r, j) * weights[1]
                part[at, j] = here + move
                at += 1

    counts = [hi - lo for lo, hi in parts]

    @pl.loop(0, sum(counts))
    def _(t):
        row = t + parts[0][0]
        if len(parts) == 2:
            row = jnp.where(t < counts[0], row, t - counts[0] + parts[1][0])
        vals = [column(src, row, j) for j in range(-3, seg + 3)]
        faces = sided(vals, ycoef, eps_xy)
        for j in range(seg):
            i = j + 3
            move = jnp.where(ymask, faces[i], faces[i - 1])
            out = part[t, j] + move + turn * turning(vals[i], eps_t)
            dst[0][row + dst[1], pl.ds(OFF + start + j, SUB, stride=seg), :] = out


def clear_columns(dst, parts, cols):
    py = lax.axis_index("py")
    for edge, begin in ((0, 0), (lax.axis_size("py") - 1, OFF + cols)):

        @pl.when(py == edge)
        def _():
            for lo, hi in parts:
                dst[0][pl.ds(lo + dst[1], hi - lo), pl.ds(begin, OFF), :] = jnp.zeros((hi - lo, OFF, LANES), jnp.float32)


def inner_kernel(const_ref, own, one, part, *, turns, gap):
    rows, wide = own.shape[:2]
    cols = wide - 2 * OFF
    parts = [(3, rows - 3)]
    stage(0, (own, 0), (one, -3), None, part, const_ref, parts, (cols, 6, gap), turns[0])
    clear_columns((one, -3), parts, cols)


def outer_kernel(const_ref, recv1_ref, recv2_ref, own, inner, one, two, send1, send2, field, part, *, turns, gap):
    rows, wide = own.shape[:2]
    cols = wide - 2 * OFF

    def write(row, col, values):
        field[row + DEPTH, pl.ds(beside(begin) + col, values.shape[0]), :] = values

    for begin, count, at in message_parts(cols):
        where = pl.ds(at, message_lines(count))
        unpack_pair(recv1_ref.at[where], recv2_ref.at[where], write, rows, count, FULL1, HALF1)
    clear_columns((field, DEPTH), [(-DEPTH, 0), (rows, rows + DEPTH)], cols)
    field[pl.ds(DEPTH, DEPTH)] = own[pl.ds(0, DEPTH)]
    field[pl.ds(rows, DEPTH)] = own[pl.ds(rows - DEPTH, DEPTH)]
    one[pl.ds(6, rows - 6)] = inner[...]
    parts = [(-3, 3), (rows - 3, rows + 3)]
    stage(0, (field, DEPTH), (one, 3), None, part, const_ref, parts, (cols, 6, gap), turns[0])
    clear_columns((one, 3), parts, cols)
    px = lax.axis_index("px")
    for edge, begin in ((0, 0), (lax.axis_size("px") - 1, 3 + rows)):

        @pl.when(px == edge)
        def _():
            one[pl.ds(begin, 3)] = jnp.zeros((3,) + one.shape[1:], jnp.float32)

    parts = [(0, 3), (rows - 3, rows)]
    stage(1, (one, 3), (two, 3), (own, 0), part, const_ref, parts, (cols, 3, gap), turns[1])
    clear_columns((two, 3), parts, cols)
    seg, start = columns_of(cols, 3)
    count = seg * SUB
    pack_pair(send1, send2, lambda r: two[r + 3, pl.ds(OFF + start, count), :], rows, count, FULL2, HALF2)


def middle_kernel(const_ref, own, one, two_in, two, three, part, *, turns, gap):
    del two_in
    rows, wide = own.shape[:2]
    cols = wide - 2 * OFF
    parts = [(3, rows - 3)]
    stage(1, (one, 3), (two, 3), (own, 0), part, const_ref, parts, (cols, 3, gap), turns[1])
    clear_columns((two, 3), parts, cols)
    stage(2, (two, 3), (three, 0), (own, 0), part, const_ref, parts, (cols, 0, gap), turns[2])


def last_kernel(const_ref, recv1_ref, recv2_ref, own, two_in, three_in, o_ref, two, three, part, *, turns, gap):
    del two_in, three_in
    rows, wide = own.shape[:2]
    cols = wide - 2 * OFF
    seg, start = columns_of(cols, 3)

    def write(row, col, values):
        two[row + 3, pl.ds(OFF + start + col, values.shape[0]), :] = values

    unpack_pair(recv1_ref, recv2_ref, write, rows, seg * SUB, FULL2, HALF2)
    parts = [(0, 3), (rows - 3, rows)]
    stage(2, (two, 3), (three, 0), (own, 0), part, const_ref, parts, (cols, 0, gap), turns[2])
    for r in range(rows):
        o_ref[pl.ds(r, LANES, stride=rows), :] = three[r, pl.ds(OFF, cols), :].T


def final_kernel(third_ref, prior_hbm, reach_ref, avoid_ref, o_hbm, held, came, gone):
    count = held.shape[0] // came.shape[0]
    part = lambda i: pl.ds(i * count, count)
    load = lambda i: pltpu.make_async_copy(prior_hbm.at[part(i)], held.at[part(i)], came.at[i])
    save = lambda i: pltpu.make_async_copy(held.at[part(i)], o_hbm.at[part(i)], gone.at[i])
    for i in range(came.shape[0]):
        load(i).start()
    reach, avoid = reach_ref[...][None], avoid_ref[...][None]
    for i in range(came.shape[0]):
        load(i).wait()
        kept = jnp.maximum(avoid, jnp.minimum(reach, third_ref[part(i)]))
        held[part(i)] = jnp.minimum(held[part(i)], kept)
        save(i).start()
    for i in range(came.shape[0]):
        save(i).wait()


def on_device(start_value, prior, reach, avoid):
    headings, rows, cols = start_value.shape
    nx, ny = lax.axis_size("px"), lax.axis_size("py")
    assert headings == LANES and cols == LANES and rows >= 2 * DEPTH and nx % 2 == 0
    gap = 2.0 * math.pi / headings
    f32 = jnp.float32
    vmem = pl.BlockSpec(memory_space=pltpu.VMEM)

    def call(kernel, outs, *args, limit=LIMIT, aliases={}, scratch=(), **kw):
        return pl.pallas_call(
            functools.partial(kernel, **kw) if kw else kernel,
            out_shape=[jax.ShapeDtypeStruct(o, f32) for o in outs],
            in_specs=[vmem] * len(args),
            out_specs=[vmem] * len(outs),
            input_output_aliases=aliases,
            scratch_shapes=[pltpu.VMEM(shape, f32) for shape in scratch],
            compiler_params=pltpu.CompilerParams(vmem_limit_bytes=limit * 2**20),
        )(*args)

    common = dict(turns=[share * time_step(gap) * TURN / (6.0 * gap) for share in SHARES], gap=gap)
    seg = columns_of(cols, 6)[0]
    wide = cols + 2 * OFF
    tall = (rows + 2 * DEPTH, wide, headings)
    short = (rows + 6, wide, headings)
    work = (max(rows - 6, 12), seg, SUB, LANES)

    sides = 1 if ny == 2 else 2
    own, table, *slabs = call(
        prep_kernel,
        [(rows, wide, headings), (len(SHARES), 16, headings)] + [(rows, OFF, headings)] * sides,
        start_value.reshape(headings * rows, cols),
    )
    blocks = call(spread_kernel, [(nx, headings // nx, rows, cols)], prior)[0]
    pairs1 = [(i, i ^ 1) for i in range(nx)]
    pairs2 = [(i, j) for i in range(nx) for j in [((i + 1) ^ 1) - 1] if 0 <= j < nx]
    if sides == 1:
        yslabs = [lax.ppermute(slabs[0], "py", [(0, 1), (1, 0)])]
    else:
        yslabs = [
            lax.ppermute(slabs[0], "py", [(i, i + 1) for i in range(ny - 1)]),
            lax.ppermute(slabs[1], "py", [(i + 1, i) for i in range(ny - 1)]),
        ]
    lines = message_lines(cols) + sides * message_lines(OFF)
    own, send1, send2 = call(
        send_kernel, [(rows, wide, headings)] + [(lines, headings)] * 2, own, yslabs[0], yslabs[-1], aliases={0: 0}
    )
    recv1 = lax.ppermute(send1, "px", pairs1)
    recv2 = lax.ppermute(send2, "px", pairs2)
    inner = call(inner_kernel, [(rows - 6, wide, headings)], table, own, scratch=[work], **common)[0]

    regrouped = lax.all_to_all(blocks, "px", split_axis=0, concat_axis=0, tiled=True)

    count = columns_of(cols, 3)[0] * SUB
    message = (FULL2 * count + HALF2 * count // 2, headings)
    one, two, send1, send2 = call(
        outer_kernel, [short, short, message, message], table, recv1, recv2, own, inner, scratch=[tall, work], **common
    )
    recv1 = lax.ppermute(send1, "px", pairs1)
    recv2 = lax.ppermute(send2, "px", pairs2)
    two, three = call(
        middle_kernel, [short, (rows, wide, headings)], table, own, one, two, aliases={3: 0}, scratch=[work], **common
    )
    third = call(
        last_kernel, [(headings * rows, cols), short, (rows, wide, headings)],
        table, recv1, recv2, own, two, three, aliases={4: 1, 5: 2}, scratch=[work], **common,
    )[0]
    pieces = 4
    return pl.pallas_call(
        final_kernel,
        out_shape=jax.ShapeDtypeStruct((headings, rows, cols), f32),
        in_specs=[vmem, pl.BlockSpec(memory_space=pl.ANY), vmem, vmem],
        out_specs=pl.BlockSpec(memory_space=pl.ANY),
        scratch_shapes=[
            pltpu.VMEM((headings, rows, cols), f32),
            pltpu.SemaphoreType.DMA((pieces,)),
            pltpu.SemaphoreType.DMA((pieces,)),
        ],
        compiler_params=pltpu.CompilerParams(vmem_limit_bytes=LIMIT * 2**20),
    )(third.reshape(headings, rows, cols), regrouped.reshape(headings, rows, cols), reach, avoid)


def solution(mesh):
    return jax.shard_map(
        on_device,
        mesh=mesh,
        in_specs=(P(None, "px", "py"), P("px", None, "py"), P("px", "py"), P("px", "py")),
        out_specs=P(None, "px", "py"),
        check_vma=False,
    )
```

```python
import functools
import math

import jax
import jax.numpy as jnp
import numpy as np
from jax import lax
from jax.experimental import pallas as pl
from jax.experimental.pallas import tpu as pltpu
from jax.sharding import PartitionSpec as P


EPS = 1e-06
SPACING = 1.0 / 64.0
SPEED = 1.0
TURN = 2.0
COURANT = 0.5
SHARES = (1.0, 0.25, 2.0 / 3.0)
LANES = 128
SUB = 8
DEPTH = 6
OFF = 16


LIMIT = 12


def ceil_div(a, b):
    return -(-a // b)


def time_step(gap):
    return COURANT / (2.0 * SPEED / SPACING + TURN / gap)


def weights_of(a, b, d, eps, want):
    bd = b * d
    ad = a * d
    ab = a * b
    mid = (bd - ad) * (2.0 / 3.0) + (ab * 0.5 + eps)
    out = []
    for name in want:
        x = {"L": mid + bd if "L" in want else None, "C": mid, "R": mid - ad if "R" in want else None}[name]
        r = inverse(x)
        out.append(r * r)
    return out


def inverse(x):
    return 1.0 / x


def sided(vals, coef, eps):
    n = len(vals)
    g, r2, r3, n1c, n3c, k1, k3 = coef
    u = [vals[i + 1] - vals[i] for i in range(n - 1)]
    w = [None] + [u[i] - u[i - 1] for i in range(1, n - 1)]
    d = [None] + [w[i + 1] - w[i] for i in range(1, n - 2)]
    tri = [None] + [weights_of(w[i], w[i + 1], d[i], eps, "LCR") for i in range(1, n - 2)]
    third = [None, None] + [d[i] - d[i - 1] for i in range(2, n - 2)]
    faces = {}
    for k in range(2, n - 3):
        m1 = tri[k - 1][0] * n1c
        m2 = tri[k][1]
        m3 = tri[k + 1][2] * n3c
        den = (m1 + m3) + m2
        num = m1 * (k1 * third[k]) + m3 * (k3 * third[k + 1])
        smooth = g * u[k] + r2 * w[k] + r3 * w[k + 1]
        faces[k] = smooth + num * inverse(den)
    return faces


def turning(vals, eps):
    n = len(vals)
    u = [vals[i + 1] - vals[i] for i in range(n - 1)]
    w = [None] + [u[i] - u[i - 1] for i in range(1, n - 1)]
    d = [None] + [w[i + 1] - w[i] for i in range(1, n - 2)]
    tri = [None] + [weights_of(w[i], w[i + 1], d[i], eps, "LCR") for i in range(1, n - 2)]
    third = [None, None] + [d[i] - d[i - 1] for i in range(2, n - 2)]
    out = []
    back = None
    for k in range(2, n - 3):
        m1 = tri[k - 1][0]
        m3 = tri[k + 1][2]
        v0 = (m1 + m3) * 0.5 + tri[k][1] * 3.0
        a1 = m1 * third[k]
        a3 = m3 * third[k + 1]
        s = w[k] + w[k + 1]
        top = u[k] * 6.0 + w[k + 1] + s
        if k > 2:
            out.append(jnp.minimum(back, (top - 3.0 * s) + (a3 + 1.5 * a1) * inverse(v0 + m1)))
        back = (a1 + 1.5 * a3) * inverse(v0 + m3) - top
    return out


def turn_blocks(flat, turned, across, result, blocks, eps, turn):
    span = LANES // SUB

    def bring(b, slot):
        tile = flat[pl.ds(pl.multiple_of(b * LANES, LANES), LANES), :].T
        across[slot, pl.ds(SUB, LANES), :] = tile
        across[slot, pl.ds(0, SUB), :] = tile[LANES - SUB :]
        across[slot, pl.ds(SUB + LANES, SUB), :] = tile[:SUB]

    def work(slot):
        vals = [across[slot, pl.ds(SUB + j, SUB, stride=span), :] for j in range(-3, span + 3)]
        for j, x in enumerate(turning(vals, eps)):
            result[slot, pl.ds(j, SUB, stride=span), :] = turn * x

    def back(b, slot):
        turned[pl.ds(pl.multiple_of(b * LANES, LANES), LANES), :] = result[slot].T

    bring(0, 0)

    @pl.loop(0, blocks // 2)
    def _(c):
        b = 2 * c
        back(jnp.maximum(b - 1, 0), 1)
        work(0)
        bring(b + 1, 1)
        back(b, 0)
        work(1)
        bring(jnp.minimum(b + 2, blocks - 1), 0)

    back(2 * (blocks // 2) - 1, 1)
    if blocks % 2:
        work(0)
        back(blocks - 1, 0)


def lanes_of(shape):
    return lax.broadcasted_iota(jnp.int32, shape, len(shape) - 1)


def fold(rows, shift):
    half = rows.shape[0] // 2
    low = pltpu.roll(rows[:half], (-shift) % LANES, 1)
    high = pltpu.roll(rows[half:], shift % LANES, 1)
    return jnp.where(lanes_of(low.shape) < LANES // 2, low, high)


def unfold(packed, shift):
    return pltpu.roll(packed, shift % LANES, 1), pltpu.roll(packed, (-shift) % LANES, 1)


QUARTER = LANES // 4
FULL1, HALF1 = 4, 2
FULL2, HALF2 = 2, 1


def even_tile():
    return lax.rem(lax.axis_index("px"), 2) == 0


def pack(ref, read, count, full, half):
    for i in range(full):
        ref[pl.ds(i * count, count), :] = read(i)[0]
    for i in range(half):
        values, shift = read(full + i)
        ref[pl.ds(full * count + i * (count // 2), count // 2), :] = fold(values, shift)


def pack_pair(one_ref, two_ref, row, rows, count, full, half):
    upper = lambda i: (row(rows - 1 - i), QUARTER)
    lower = lambda i: (row(i), -QUARTER)

    @pl.when(even_tile())
    def _():
        pack(one_ref, upper, count, full, half)
        pack(two_ref, lower, count, full, half)

    @pl.when(jnp.logical_not(even_tile()))
    def _():
        pack(one_ref, lower, count, full, half)
        pack(two_ref, upper, count, full, half)


def unpack_pair(one_ref, two_ref, write, rows, count, full, half):
    def unpack(ref, low):
        at = lambda i: -1 - i if low else rows + i
        for i in range(full):
            write(at(i), 0, ref[pl.ds(i * count, count), :])
        for i in range(half):
            packed = ref[pl.ds(full * count + i * (count // 2), count // 2), :]
            first, second = unfold(packed, QUARTER if low else -QUARTER)
            write(at(full + i), 0, first)
            write(at(full + i), count // 2, second)

    @pl.when(even_tile())
    def _():
        unpack(one_ref, False)
        unpack(two_ref, True)

    @pl.when(jnp.logical_not(even_tile()))
    def _():
        unpack(one_ref, True)
        unpack(two_ref, False)


def fill_table(table_ref):
    headings = table_ref.shape[2]
    gap = 2.0 * math.pi / headings
    lane = lax.broadcasted_iota(jnp.int32, (SUB, headings), 1)
    angle = lane.astype(jnp.float32) * np.float32(gap)
    behind_x = (lane >= headings // 4) & (lane < 3 * headings // 4)
    for stage_index, share in enumerate(SHARES):
        step = share * time_step(gap) * SPEED / SPACING
        for at, wave, back in ((0, jnp.cos(angle), behind_x), (8, jnp.sin(angle), lane > headings // 2)):
            g = wave * np.float32(step)
            rows = [
                g,
                g * jnp.where(back, 1.0 / 6.0, -1.0 / 3.0),
                g * jnp.where(back, 1.0 / 3.0, -1.0 / 6.0),
                jnp.where(back, 1.0 / 6.0, 0.5),
                jnp.where(back, 0.5, 1.0 / 6.0),
                g * jnp.where(back, -1.0 / 3.0, 1.0 / 6.0),
                g * jnp.where(back, -1.0 / 6.0, 1.0 / 3.0),
                jnp.where(back, 0.0, 1.0),
            ]
            for i, values in enumerate(rows):
                table_ref[stage_index, pl.ds(at + i, 1), :] = values[:1]


def prep_kernel(x_ref, own_ref, table_ref, *slabs):
    rows = own_ref.shape[0]
    cols = x_ref.shape[1]
    fill_table(table_ref)
    for r in range(rows):
        own_ref[r, pl.ds(OFF, cols), :] = x_ref[pl.ds(r, LANES, stride=rows), :].T

    def cut(ref, begin):
        ref[...] = own_ref[:, pl.ds(begin, OFF), :]

    if len(slabs) == 1:
        pl.when(lax.axis_index("py") == 0)(lambda: cut(slabs[0], cols))
        pl.when(lax.axis_index("py") != 0)(lambda: cut(slabs[0], OFF))
    else:
        cut(slabs[0], cols)
        cut(slabs[1], OFF)


def spread_kernel(p_ref, o_ref):
    rows = o_ref.shape[2]
    for i in range(o_ref.shape[0]):
        o_ref[i] = p_ref[:, pl.ds(i * rows, rows), :]


def send_kernel(own_in, ylow_ref, yhigh_ref, own, one_ref, two_ref):
    del own_in
    rows, wide = own.shape[:2]
    cols = wide - 2 * OFF
    own[:, pl.ds(0, OFF), :] = ylow_ref[...]
    own[:, pl.ds(OFF + cols, OFF), :] = yhigh_ref[...]
    clear_columns((own, 0), [(0, rows)], cols)
    for begin, count, at in message_parts(cols):
        read = lambda r: own[r, pl.ds(beside(begin), count), :]
        where = pl.ds(at, message_lines(count))
        pack_pair(one_ref.at[where], two_ref.at[where], read, rows, count, FULL1, HALF1)


def message_parts(cols):
    begins = [0, -OFF, cols]
    if lax.axis_size("py") == 2:
        begins = [0, pl.multiple_of(jnp.where(lax.axis_index("py") == 0, cols, -OFF), OFF)]
    parts, at = [], 0
    for begin in begins:
        count = OFF if parts else cols
        parts.append((begin, count, at))
        at += message_lines(count)
    return parts


def beside(begin):
    return OFF + begin if isinstance(begin, int) else pl.multiple_of(OFF + begin, OFF)


def message_lines(count):
    return FULL1 * count + HALF1 * (count // 2)


def columns_of(cols, margin):
    seg = ceil_div(cols + 2 * margin, SUB)
    if seg % SUB == 0:
        seg += 1
    return seg, -((seg * SUB - cols) // 2)


def stage(index, src, dst, base, part, const_ref, parts, sizes, turn):
    cols, margin, gap = sizes
    seg, start = columns_of(cols, margin)
    eps_xy = 0.5 * EPS * SPACING**2
    eps_t = 0.5 * EPS * gap**2
    part, flat, turned, across, result = part
    weights = (None, (0.25, 0.75), (2.0 / 3.0, 1.0 / 3.0))[index]

    def column(array, row, j):
        return array[0][row + array[1], pl.ds(OFF + start + j, SUB, stride=seg), :]

    def const(i):
        return const_ref[index, pl.ds(i, SUB, stride=0), :]

    xcoef = [const(i) for i in range(7)]
    ycoef = [const(i) for i in range(8, 15)]
    xmask = const(7) > 0.5
    ymask = const(15) > 0.5

    @pl.loop(0, seg)
    def _(j):
        at = 0
        for lo, hi in parts:
            vals = [column(src, r, j) for r in range(lo - 3, hi + 3)]
            faces = sided(vals, xcoef, eps_xy)
            for r in range(lo, hi):
                i = r - lo + 3
                move = jnp.where(xmask, faces[i], faces[i - 1])
                here = vals[i]
                if weights is not None:
                    here = here * weights[0] + column(base, r, j) * weights[1]
                part[at, j] = here + move
                flat[pl.ds(at * seg * SUB + j, SUB, stride=seg), :] = vals[i]
                at += 1

    counts = [hi - lo for lo, hi in parts]
    turn_blocks(flat, turned, across, result, ceil_div(sum(counts) * seg * SUB, LANES), eps_t, turn)

    @pl.loop(0, sum(counts))
    def _(t):
        row = t + parts[0][0]
        if len(parts) == 2:
            row = jnp.where(t < counts[0], row, t - counts[0] + parts[1][0])
        vals = [column(src, row, j) for j in range(-3, seg + 3)]
        faces = sided(vals, ycoef, eps_xy)
        for j in range(seg):
            i = j + 3
            move = jnp.where(ymask, faces[i], faces[i - 1])
            out = part[t, j] + move + turned[pl.ds(t * seg * SUB + j, SUB, stride=seg), :]
            dst[0][row + dst[1], pl.ds(OFF + start + j, SUB, stride=seg), :] = out


def clear_columns(dst, parts, cols):
    py = lax.axis_index("py")
    for edge, begin in ((0, 0), (lax.axis_size("py") - 1, OFF + cols)):

        @pl.when(py == edge)
        def _():
            for lo, hi in parts:
                dst[0][pl.ds(lo + dst[1], hi - lo), pl.ds(begin, OFF), :] = jnp.zeros((hi - lo, OFF, LANES), jnp.float32)


def inner_kernel(const_ref, own, one, *part, turns, gap):
    rows, wide = own.shape[:2]
    cols = wide - 2 * OFF
    parts = [(3, rows - 3)]
    stage(0, (own, 0), (one, -3), None, part, const_ref, parts, (cols, 6, gap), turns[0])
    clear_columns((one, -3), parts, cols)


def outer_kernel(const_ref, recv1_ref, recv2_ref, own, inner, one, two, send1, send2, field, *part, turns, gap):
    rows, wide = own.shape[:2]
    cols = wide - 2 * OFF

    def write(row, col, values):
        field[row + DEPTH, pl.ds(beside(begin) + col, values.shape[0]), :] = values

    for begin, count, at in message_parts(cols):
        where = pl.ds(at, message_lines(count))
        unpack_pair(recv1_ref.at[where], recv2_ref.at[where], write, rows, count, FULL1, HALF1)
    clear_columns((field, DEPTH), [(-DEPTH, 0), (rows, rows + DEPTH)], cols)
    field[pl.ds(DEPTH, DEPTH)] = own[pl.ds(0, DEPTH)]
    field[pl.ds(rows, DEPTH)] = own[pl.ds(rows - DEPTH, DEPTH)]
    one[pl.ds(6, rows - 6)] = inner[...]
    parts = [(-3, 3), (rows - 3, rows + 3)]
    stage(0, (field, DEPTH), (one, 3), None, part, const_ref, parts, (cols, 6, gap), turns[0])
    clear_columns((one, 3), parts, cols)
    px = lax.axis_index("px")
    for edge, begin in ((0, 0), (lax.axis_size("px") - 1, 3 + rows)):

        @pl.when(px == edge)
        def _():
            one[pl.ds(begin, 3)] = jnp.zeros((3,) + one.shape[1:], jnp.float32)

    parts = [(0, 3), (rows - 3, rows)]
    stage(1, (one, 3), (two, 3), (own, 0), part, const_ref, parts, (cols, 3, gap), turns[1])
    clear_columns((two, 3), parts, cols)
    seg, start = columns_of(cols, 3)
    count = seg * SUB
    pack_pair(send1, send2, lambda r: two[r + 3, pl.ds(OFF + start, count), :], rows, count, FULL2, HALF2)


def middle_kernel(const_ref, own, one, two_in, two, three, *part, turns, gap):
    del two_in
    rows, wide = own.shape[:2]
    cols = wide - 2 * OFF
    parts = [(3, rows - 3)]
    stage(1, (one, 3), (two, 3), (own, 0), part, const_ref, parts, (cols, 3, gap), turns[1])
    clear_columns((two, 3), parts, cols)
    stage(2, (two, 3), (three, 0), (own, 0), part, const_ref, parts, (cols, 0, gap), turns[2])


def last_kernel(const_ref, recv1_ref, recv2_ref, own, two_in, three_in, o_ref, two, three, *part, turns, gap):
    del two_in, three_in
    rows, wide = own.shape[:2]
    cols = wide - 2 * OFF
    seg, start = columns_of(cols, 3)

    def write(row, col, values):
        two[row + 3, pl.ds(OFF + start + col, values.shape[0]), :] = values

    unpack_pair(recv1_ref, recv2_ref, write, rows, seg * SUB, FULL2, HALF2)
    parts = [(0, 3), (rows - 3, rows)]
    stage(2, (two, 3), (three, 0), (own, 0), part, const_ref, parts, (cols, 0, gap), turns[2])
    for r in range(rows):
        o_ref[pl.ds(r, LANES, stride=rows), :] = three[r, pl.ds(OFF, cols), :].T


def final_kernel(third_ref, prior_hbm, reach_ref, avoid_ref, o_hbm, held, came, gone):
    count = held.shape[0] // came.shape[0]
    part = lambda i: pl.ds(i * count, count)
    load = lambda i: pltpu.make_async_copy(prior_hbm.at[part(i)], held.at[part(i)], came.at[i])
    save = lambda i: pltpu.make_async_copy(held.at[part(i)], o_hbm.at[part(i)], gone.at[i])
    for i in range(came.shape[0]):
        load(i).start()
    reach, avoid = reach_ref[...][None], avoid_ref[...][None]
    for i in range(came.shape[0]):
        load(i).wait()
        kept = jnp.maximum(avoid, jnp.minimum(reach, third_ref[part(i)]))
        held[part(i)] = jnp.minimum(held[part(i)], kept)
        save(i).start()
    for i in range(came.shape[0]):
        save(i).wait()


def on_device(start_value, prior, reach, avoid):
    headings, rows, cols = start_value.shape
    nx, ny = lax.axis_size("px"), lax.axis_size("py")
    assert headings == LANES and cols == LANES and rows >= 2 * DEPTH and nx % 2 == 0
    gap = 2.0 * math.pi / headings
    f32 = jnp.float32
    vmem = pl.BlockSpec(memory_space=pltpu.VMEM)

    def call(kernel, outs, *args, limit=LIMIT, aliases={}, scratch=(), **kw):
        return pl.pallas_call(
            functools.partial(kernel, **kw) if kw else kernel,
            out_shape=[jax.ShapeDtypeStruct(o, f32) for o in outs],
            in_specs=[vmem] * len(args),
            out_specs=[vmem] * len(outs),
            input_output_aliases=aliases,
            scratch_shapes=[pltpu.VMEM(shape, f32) for shape in scratch],
            compiler_params=pltpu.CompilerParams(vmem_limit_bytes=limit * 2**20),
        )(*args)

    common = dict(turns=[share * time_step(gap) * TURN / (6.0 * gap) for share in SHARES], gap=gap)
    seg = columns_of(cols, 6)[0]
    wide = cols + 2 * OFF
    tall = (rows + 2 * DEPTH, wide, headings)
    short = (rows + 6, wide, headings)
    most = max(rows - 6, 12)
    lines = ceil_div(most * seg * SUB, LANES) * LANES
    work = [
        (most, seg, SUB, LANES),
        (lines, LANES),
        (lines, LANES),
        (2, LANES + 2 * SUB, LANES),
        (2, LANES, LANES),
    ]

    sides = 1 if ny == 2 else 2
    own, table, *slabs = call(
        prep_kernel,
        [(rows, wide, headings), (len(SHARES), 16, headings)] + [(rows, OFF, headings)] * sides,
        start_value.reshape(headings * rows, cols),
    )
    blocks = call(spread_kernel, [(nx, headings // nx, rows, cols)], prior)[0]
    pairs1 = [(i, i ^ 1) for i in range(nx)]
    pairs2 = [(i, j) for i in range(nx) for j in [((i + 1) ^ 1) - 1] if 0 <= j < nx]
    if sides == 1:
        yslabs = [lax.ppermute(slabs[0], "py", [(0, 1), (1, 0)])]
    else:
        yslabs = [
            lax.ppermute(slabs[0], "py", [(i, i + 1) for i in range(ny - 1)]),
            lax.ppermute(slabs[1], "py", [(i + 1, i) for i in range(ny - 1)]),
        ]
    length = message_lines(cols) + sides * message_lines(OFF)
    own, send1, send2 = call(
        send_kernel, [(rows, wide, headings)] + [(length, headings)] * 2, own, yslabs[0], yslabs[-1], aliases={0: 0}
    )
    recv1 = lax.ppermute(send1, "px", pairs1)
    recv2 = lax.ppermute(send2, "px", pairs2)
    inner = call(inner_kernel, [(rows - 6, wide, headings)], table, own, scratch=work, **common)[0]

    regrouped = lax.all_to_all(blocks, "px", split_axis=0, concat_axis=0, tiled=True)

    count = columns_of(cols, 3)[0] * SUB
    message = (FULL2 * count + HALF2 * count // 2, headings)
    one, two, send1, send2 = call(
        outer_kernel, [short, short, message, message], table, recv1, recv2, own, inner, scratch=[tall] + work, **common
    )
    recv1 = lax.ppermute(send1, "px", pairs1)
    recv2 = lax.ppermute(send2, "px", pairs2)
    two, three = call(
        middle_kernel, [short, (rows, wide, headings)], table, own, one, two, aliases={3: 0}, scratch=work, **common
    )
    third = call(
        last_kernel, [(headings * rows, cols), short, (rows, wide, headings)],
        table, recv1, recv2, own, two, three, aliases={4: 1, 5: 2}, scratch=work, **common,
    )[0]
    pieces = 4
    return pl.pallas_call(
        final_kernel,
        out_shape=jax.ShapeDtypeStruct((headings, rows, cols), f32),
        in_specs=[vmem, pl.BlockSpec(memory_space=pl.ANY), vmem, vmem],
        out_specs=pl.BlockSpec(memory_space=pl.ANY),
        scratch_shapes=[
            pltpu.VMEM((headings, rows, cols), f32),
            pltpu.SemaphoreType.DMA((pieces,)),
            pltpu.SemaphoreType.DMA((pieces,)),
        ],
        compiler_params=pltpu.CompilerParams(vmem_limit_bytes=LIMIT * 2**20),
    )(third.reshape(headings, rows, cols), regrouped.reshape(headings, rows, cols), reach, avoid)


def solution(mesh):
    return jax.shard_map(
        on_device,
        mesh=mesh,
        in_specs=(P(None, "px", "py"), P("px", None, "py"), P("px", "py"), P("px", "py")),
        out_specs=P(None, "px", "py"),
        check_vma=False,
    )
```
